256 devices in a mesh: section: 4 (over y), dp: 16 (over z, core), tensor: 4 (over x).
Axes of the slice: x: 4, y: 4, z: 8, core: 2. Of those that a mesh axis runs over, the one named last changes fastest.
Arguments:
- hidden_in: bfloat16 [4096, 5120], P('dp', 'tensor'), may hold values from -6 to 6
- kv_cache: bfloat16 [4, 16, 2, 1024, 512], P('section', 'dp', None, None, 'tensor'), may hold values from -512 to 512
- norm_gain: float32 [4, 5120], P('section'), may hold values from 0.25 to 1.75
- w_query: bfloat16 [4, 5120, 2560], P('section', 'dp', 'tensor'), may hold values from -0.078125 to 0.078125
- w_keyval: bfloat16 [4, 5120, 2, 512], P('section', 'dp', None, 'tensor'), may hold values from -0.078125 to 0.078125
- w_out: bfloat16 [4, 2560, 5120], P('section', 'tensor', 'dp'), may hold values from -1.1953125 to 1.1953125
- stretch_count: int32 [16], P('dp'), may hold values from 1 to 2, 24 in all
- prefix_len: int32 [16], P('dp'), may hold values from 1 to 1024, 8704 in all
Outputs:
- attn_out: bfloat16 [4, 4096, 5120], P('section', 'dp', 'tensor')
- hidden_out: bfloat16 [4, 4096, 5120], P('section', 'dp', 'tensor')
The draws below stay inside these ranges and needn't reach their ends.
Inputs may be any that keep to these rules, and one draw needn't show every extreme that they name: `stretch_count`: some transcript has 2 live stretches. `prefix_len`: some transcript keeps 1024 rows.
All inputs are finite; a program needn't handle non-finite values. No bound on the sum of `stretch_count` or of `prefix_len` on one device may be relied on, other than what follows from the above.
Results may differ from the reference program's by a relative error of at most 0.02.
Values may be sent and summed in bfloat16 or wider, within the bound.
No kernel may reach another device: no remote copies, remote signals or barrier semaphores. Data moves between devices by JAX's collectives and lax.ppermute only.
A program may use at most 128 MiB of HBM per device.

```python
import math
import jax
import jax.numpy as jnp
import numpy as np
from jax import lax

D = 5120
HEADS = 20
KV_HEADS = 4
HEAD_DIM = 128
STRETCH = 128
SLOTS = 2
PREFIX = 1024
GROUPS = 16
N_SECTION = 4
N_TENSOR = 4


def draw_kv_cache(key, part):
    rand_keys = jax.random.split(key, 6)
    full_shape = (N_SECTION, GROUPS, 2, PREFIX, KV_HEADS * HEAD_DIM)
    section_index = jnp.arange(N_SECTION, dtype=jnp.int32)[:, None, None, None]
    bulk_draw = jax.random.truncated_normal(rand_keys[0], -6.0, 6.0, full_shape, jnp.float32)
    strength = jnp.exp(jax.random.uniform(rand_keys[1], (N_SECTION, GROUPS, 1, 1), jnp.float32, math.log(40.0), math.log(160.0)))
    drawn = jnp.exp(jax.random.uniform(rand_keys[5], (N_SECTION, GROUPS, 1, 1), jnp.float32, math.log(2.0), math.log(4.0)))
    strength = jnp.where(section_index == 0, strength, drawn)
    head_pick = jax.random.randint(rand_keys[2], (N_SECTION, GROUPS, 1, 1), 0, KV_HEADS)
    lead_dir = jax.random.truncated_normal(rand_keys[3], -3.0, 3.0, (N_SECTION, GROUPS, 2, HEAD_DIM), jnp.float32)
    nudge_dir = 2.0 * jax.random.truncated_normal(rand_keys[4], -3.0, 3.0, (N_SECTION, GROUPS, 2, HEAD_DIM), jnp.float32)
    level_mult = jnp.array([1.0, 0.4], jnp.float32)
    strong_rows = strength * level_mult[None, None, :, None] * lead_dir
    special_rows = jnp.stack([strong_rows[:, :, 0], strong_rows[:, :, 0] + nudge_dir[:, :, 0], strong_rows[:, :, 1], strong_rows[:, :, 1] + nudge_dir[:, :, 1]], axis=2)
    special_rows = jnp.tile(special_rows, (1, 1, 1, KV_HEADS))
    special_rows = jnp.concatenate([special_rows, jnp.zeros((N_SECTION, GROUPS, PREFIX - 4, KV_HEADS * HEAD_DIM), jnp.float32)], axis=2)
    row_index = jnp.arange(PREFIX, dtype=jnp.int32)[None, None, :, None]
    col_index = jnp.arange(KV_HEADS * HEAD_DIM, dtype=jnp.int32)[None, None, None, :]
    head_index = col_index // HEAD_DIM
    chosen_cells = (row_index < 4) & (head_index == head_pick)
    key_plane = jnp.clip(jnp.where(chosen_cells, special_rows, bulk_draw[:, :, 0]), -512.0, 512.0)
    group_index = jnp.arange(GROUPS, dtype=jnp.int32)[None, :, None, None]
    corner_block = (section_index == 0) & (group_index == 0)
    top_col = head_pick[0, 0, 0, 0] * HEAD_DIM
    key_plane = jnp.where(corner_block & (row_index == 0) & (col_index == top_col), 512.0, key_plane)
    key_plane = jnp.where(corner_block & (row_index == 2) & (col_index == top_col + 1), -512.0, key_plane)
    result = jnp.stack([key_plane, bulk_draw[:, :, 1]], axis=2)
    return result.astype(jnp.bfloat16)


def block_levels(key, dims, cuts, low, top_value):
    def one(dim, parts):
        draws = jax.random.uniform(jax.random.fold_in(jax.random.fold_in(key, 6), dim), (parts,), jnp.float32, low / len(cuts), top_value / len(cuts))
        return jnp.repeat(jnp.exp(draws), dims[dim] // parts).reshape((-1,) + (1,) * (len(dims) - dim - 1))

    level = one(*cuts[0])
    for cut in cuts[1:]:
        level = level * one(*cut)
    return level


def split_up(amount, total, limit, slope):
    loads = [(1 << 20) // math.isqrt(grade ** slope) + 1 for grade in range(2, amount + 1)]
    surplus, given = total - limit - (amount - 1), [1] * (amount - 1)
    while surplus > 0:
        movable = [i for i in range(amount - 1) if given[i] < limit]
        pool, budget = sum([loads[i] for i in movable]), surplus
        for i in movable:
            addition = min(limit - given[i], max(1, budget * loads[i] // pool), surplus)
            given[i] = given[i] + addition
            surplus = surplus - addition
    return np.array([limit] + given)


def uneven_parts(own_key, count, total, bound, slope):
    if count == 2:
        one = jax.random.randint(own_key, (), max(1, total - bound), min(bound, total - 1) + 1)
        return jnp.stack([one, total - one])
    tallies = jnp.asarray(split_up(count, total, bound, slope), jnp.int32)
    pairs = (count - 1) // 2
    giver, sink = tallies[1:1 + 2 * pairs:2], tallies[2:2 + 2 * pairs:2]
    slack = jnp.minimum(giver - 1, bound - sink)
    passed = jax.random.randint(jax.random.fold_in(own_key, 1), (pairs,), 0, 1 << 20) % (slack + 1)
    tallies = tallies.at[1:1 + 2 * pairs:2].set(giver - passed).at[2:2 + 2 * pairs:2].set(sink + passed)
    return tallies[jax.random.permutation(jax.random.fold_in(own_key, 2), count)]


def bell_draw(rng, shape, width, bound, cuts=(), held_as=jnp.bfloat16):
    factor_of = block_levels(rng, shape, cuts, -0.22, 0.18) if cuts else 1.0
    drawn = jax.random.normal(rng, shape, jnp.float32) * width * factor_of
    return jnp.minimum(jnp.maximum(drawn, -bound), bound).astype(held_as)


def setup_inputs(seed: int = 0) -> dict:
    streams_of = jax.random.split(jax.random.key(seed), 9)
    return {
        "hidden_in": bell_draw(streams_of[0], (GROUPS * SLOTS * STRETCH, D), 1.0, 6.0, ((0, 16), (1, 4))),
        "kv_cache": draw_kv_cache(jax.random.fold_in(streams_of[8], 71), 0),
        "norm_gain": jnp.clip(1.0 + 0.15 * jax.random.normal(streams_of[2], (N_SECTION, D), jnp.float32), 0.25, 1.75),
        "w_query": bell_draw(streams_of[3], (N_SECTION, D, HEADS * HEAD_DIM), D ** -0.5, 0.078125, ((0, 4), (1, 16), (2, 4))),
        "w_keyval": bell_draw(streams_of[4], (N_SECTION, D, 2, KV_HEADS * HEAD_DIM), D ** -0.5, 0.078125, ((0, 4), (1, 16), (3, 4))),
        "w_out": bell_draw(streams_of[5], (N_SECTION, HEADS * HEAD_DIM, D), 0.2, 1.1953125, ((0, 4), (1, 4), (2, 16))),
        "stretch_count": uneven_parts(streams_of[6], GROUPS, GROUPS * (SLOTS + 1) // 2, SLOTS, 2).astype(jnp.int32),
        "prefix_len": uneven_parts(streams_of[7], GROUPS, (GROUPS + 1) * PREFIX // 2, PREFIX, 1).astype(jnp.int32),
    }


theta_base = 1000000.0
eps_norm = 1e-06
masked_score = -1e+30

def rotary(values, positions):
    half_dim = values.shape[-1] // 2
    inv_freq = theta_base ** (-(jnp.arange(half_dim, dtype=jnp.float32) * 2.0 / values.shape[-1]))
    angles = positions.astype(jnp.float32)[:, None] * inv_freq[None, :]
    cosine = jnp.cos(angles)[:, None, :]
    sine_part = jnp.sin(angles)[:, None, :]
    first_half = values[..., :half_dim]
    second_half = values[..., half_dim:]
    return jnp.concatenate([first_half * cosine - second_half * sine_part, second_half * cosine + first_half * sine_part], axis=-1)

def group_layer(x_group, kv_store, prefix, gain_vec, query_w, keyval_w, out_w):
    row_total = x_group.shape[0]
    x_float = x_group.astype(jnp.float32)
    normed = (x_float * lax.rsqrt(lax.optimization_barrier(jnp.mean(x_float * x_float, axis=1, keepdims=True)) + eps_norm) * gain_vec[None, :]).astype(jnp.bfloat16)
    positions = prefix + jnp.arange(row_total, dtype=jnp.int32)
    query_vec = jnp.dot(normed, query_w, preferred_element_type=jnp.float32).reshape(row_total, HEADS, HEAD_DIM)
    query_vec = rotary(query_vec, positions)
    keyval = jnp.dot(normed, keyval_w.reshape(D, 2 * KV_HEADS * HEAD_DIM), preferred_element_type=jnp.float32)
    key_new = rotary(keyval[:, :KV_HEADS * HEAD_DIM].reshape(row_total, KV_HEADS, HEAD_DIM), positions).astype(jnp.bfloat16)
    value_new = keyval[:, KV_HEADS * HEAD_DIM:].reshape(row_total, KV_HEADS, HEAD_DIM).astype(jnp.bfloat16)
    all_keys = jnp.concatenate([kv_store[0].reshape(PREFIX, KV_HEADS, HEAD_DIM), key_new], axis=0)
    all_vals = jnp.concatenate([kv_store[1].reshape(PREFIX, KV_HEADS, HEAD_DIM), value_new], axis=0)
    group_size = HEADS // KV_HEADS
    query_grp = query_vec.reshape(row_total, KV_HEADS, group_size, HEAD_DIM).astype(jnp.float32)
    scores = jnp.einsum('rkgd,jkd->kgrj', query_grp, all_keys.astype(jnp.float32), precision=lax.Precision.HIGHEST) * HEAD_DIM ** (-0.5)
    key_pos = jnp.arange(PREFIX + row_total, dtype=jnp.int32)
    row_pos = jnp.arange(row_total, dtype=jnp.int32)
    allowed = jnp.where(key_pos[None, :] < PREFIX, (key_pos < prefix)[None, :], key_pos[None, :] - PREFIX <= row_pos[:, None])
    scores = jnp.where(allowed[None, None], scores, masked_score)
    row_max = lax.optimization_barrier(jnp.max(scores, axis=-1, keepdims=True))
    expd = jnp.exp(scores - row_max)
    probs = (expd / lax.optimization_barrier(jnp.sum(expd, axis=-1, keepdims=True))).astype(jnp.bfloat16)
    mixed_heads = jnp.einsum('kgrj,jkd->rkgd', probs.astype(jnp.float32), all_vals.astype(jnp.float32))
    mixed_heads = mixed_heads.reshape(row_total, HEADS * HEAD_DIM).astype(jnp.bfloat16)
    local_cols = HEADS * HEAD_DIM // N_TENSOR
    partials = jnp.einsum('rtc,tcd->trd', mixed_heads.reshape(row_total, N_TENSOR, local_cols).astype(jnp.float32), out_w.reshape(N_TENSOR, local_cols, D).astype(jnp.float32))
    rounded = lax.optimization_barrier(partials.astype(jnp.bfloat16))
    attn = lax.optimization_barrier(jnp.sum(rounded.astype(jnp.float32), axis=0))
    return (attn.astype(jnp.bfloat16), (x_float + attn).astype(jnp.bfloat16))

def reference(hidden_in, kv_cache, norm_gain, w_query, w_keyval, w_out, stretch_count, prefix_len):
    row_total = SLOTS * STRETCH
    x_now = hidden_in.reshape(GROUPS, row_total, D)
    live_mask = ((jnp.arange(row_total, dtype=jnp.int32) // STRETCH)[None, :] < stretch_count[:, None])[:, :, None]
    attn_list = []
    hidden_list = []
    for section_num in range(N_SECTION):

        def per_group(items, section_num=section_num):
            x_group, kv_store, prefix = items
            return group_layer(x_group, kv_store, prefix, norm_gain[section_num], w_query[section_num], w_keyval[section_num], w_out[section_num])
        attn_vals, hid_vals = lax.map(per_group, (x_now, kv_cache[section_num], prefix_len))
        attn_list.append(jnp.where(live_mask, attn_vals, jnp.zeros_like(attn_vals)).reshape(GROUPS * row_total, D))
        hidden_list.append(jnp.where(live_mask, hid_vals, jnp.zeros_like(hid_vals)).reshape(GROUPS * row_total, D))
        x_now = hid_vals
    return (jnp.stack(attn_list, axis=0), jnp.stack(hidden_list, axis=0))
```

```python
import jax
import jax.numpy as jnp
from jax import lax
from jax.experimental import pallas as pl
from jax.experimental.pallas import tpu as pltpu
from jax.sharding import PartitionSpec as P

HEAD_DIM = 128
STRETCH = 128
SUBS = 1

theta_base = 1000000.0
eps_norm = 1e-06
masked_score = -1e30


def shift(value, axis, steps):
    count = lax.axis_size(axis)
    return lax.ppermute(value, axis, [(i, (i + steps) % count) for i in range(count)])


def spread(value, axis):
    return [value] + [shift(value, axis, k) for k in range(1, lax.axis_size(axis))]


def attend_kernel(
    scal, x0, x1, x2, x3, gain, cos_t, sin_t, kv, kin, vin, w_hbm,
    heads, kout, vout, w_vm, q_vm, k2_vm, sems,
):
    pieces = (x0, x1, x2, x3)
    rows, part = x0.shape
    copies = []
    for k in range(4):
        src = pl.multiple_of(scal[2 + k] * part, part)
        cp = pltpu.make_async_copy(w_hbm.at[pl.ds(src, part), :], w_vm.at[k], sems.at[k])
        cp.start()
        copies.append(cp)
    row0 = pl.multiple_of(scal[0], rows)
    prefix = scal[1]
    total = None
    for k in range(4):
        xf = pieces[k][...].astype(jnp.float32)
        part_sum = jnp.sum(xf * xf, axis=1, keepdims=True)
        total = part_sum if total is None else total + part_sum
    scale = lax.rsqrt(total / (4 * part) + eps_norm)
    acc = None
    for k in range(4):
        normed = (pieces[k][...].astype(jnp.float32) * scale * gain[k]).astype(jnp.bfloat16)
        copies[k].wait()
        term = jnp.dot(normed, w_vm[k], preferred_element_type=jnp.float32)
        acc = term if acc is None else acc + term
    cosv = cos_t[pl.ds(row0, rows), :]
    sinv = sin_t[pl.ds(row0, rows), :]
    n_heads = heads.shape[1] // HEAD_DIM

    def rot(v):
        return v * cosv + pltpu.roll(v, HEAD_DIM // 2, 1) * sinv

    for h in range(n_heads):
        qh = rot(acc[:, h * HEAD_DIM : (h + 1) * HEAD_DIM]) * (HEAD_DIM**-0.5)
        hi = qh.astype(jnp.bfloat16)
        rem = qh - hi.astype(jnp.float32)
        mid = rem.astype(jnp.bfloat16)
        low = (rem - mid.astype(jnp.float32)).astype(jnp.bfloat16)
        q_vm[h, :, :HEAD_DIM] = hi
        q_vm[h, :, HEAD_DIM : 2 * HEAD_DIM] = mid
        q_vm[h, :, 2 * HEAD_DIM :] = low
    base = n_heads * HEAD_DIM
    kout[...] = kin[...]
    vout[...] = vin[...]
    kout[pl.ds(row0, rows), :] = rot(acc[:, base : base + HEAD_DIM]).astype(jnp.bfloat16)
    vout[pl.ds(row0, rows), :] = acc[:, base + HEAD_DIM :].astype(jnp.bfloat16)
    cap = kv.shape[1]
    new_rows = kin.shape[0]
    for j in range(3):
        k2_vm[:cap, j * HEAD_DIM : (j + 1) * HEAD_DIM] = kv[0]
        k2_vm[cap:, j * HEAD_DIM : (j + 1) * HEAD_DIM] = kout[...]
    kept_ok = lax.broadcasted_iota(jnp.int32, (rows, cap), 1) < prefix
    new_ok = lax.broadcasted_iota(jnp.int32, (rows, new_rows), 1) <= (
        row0 + lax.broadcasted_iota(jnp.int32, (rows, new_rows), 0)
    )
    nt = (((1,), (1,)), ((), ()))
    for h in range(n_heads):
        qh = q_vm[h]
        s1 = lax.dot_general(qh, k2_vm[:cap], nt, preferred_element_type=jnp.float32)
        s2 = lax.dot_general(qh, k2_vm[cap:], nt, preferred_element_type=jnp.float32)
        s1 = jnp.where(kept_ok, s1, masked_score)
        s2 = jnp.where(new_ok, s2, masked_score)
        top = jnp.maximum(
            jnp.max(s1, axis=1, keepdims=True), jnp.max(s2, axis=1, keepdims=True)
        )
        e1 = jnp.exp(s1 - top)
        e2 = jnp.exp(s2 - top)
        den = jnp.sum(e1, axis=1, keepdims=True) + jnp.sum(e2, axis=1, keepdims=True)
        out = jnp.dot(e1.astype(jnp.bfloat16), kv[1], preferred_element_type=jnp.float32)
        out = out + jnp.dot(e2.astype(jnp.bfloat16), vout[...], preferred_element_type=jnp.float32)
        heads[:, h * HEAD_DIM : (h + 1) * HEAD_DIM] = (out / den).astype(jnp.bfloat16)


def attend(scal, pieces, gain, cos_t, sin_t, kv, kin, vin, w):
    rows, part = pieces[0].shape
    cols = w.shape[1]
    n_heads = cols // HEAD_DIM - 2
    vm = pl.BlockSpec(memory_space=pltpu.VMEM)
    flops = 2 * rows * (4 * part * cols + 4 * n_heads * HEAD_DIM * (kv.shape[1] + kin.shape[0]))
    return pl.pallas_call(
        attend_kernel,
        out_shape=(
            jax.ShapeDtypeStruct((rows, n_heads * HEAD_DIM), jnp.bfloat16),
            jax.ShapeDtypeStruct(kin.shape, jnp.bfloat16),
            jax.ShapeDtypeStruct(vin.shape, jnp.bfloat16),
        ),
        in_specs=[pl.BlockSpec(memory_space=pltpu.SMEM)]
        + [vm] * 10
        + [pl.BlockSpec(memory_space=pl.ANY)],
        out_specs=(vm, vm, vm),
        scratch_shapes=[
            pltpu.VMEM((4, part, cols), jnp.bfloat16),
            pltpu.VMEM((n_heads, rows, 3 * HEAD_DIM), jnp.bfloat16),
            pltpu.VMEM((kv.shape[1] + kin.shape[0], 3 * HEAD_DIM), jnp.bfloat16),
            pltpu.SemaphoreType.DMA((4,)),
        ],
        compiler_params=pltpu.CompilerParams(vmem_limit_bytes=40 * 2**20),
        cost_estimate=pl.CostEstimate(
            flops=flops, bytes_accessed=2 * 4 * part * cols, transcendentals=0
        ),
        name="attend",
    )(scal, *pieces, gain, cos_t, sin_t, kv, kin, vin, w)


def project_kernel(
    scal, h0, h1, h2, h3, own, hid_in, g_hbm, attn_in, hidden_in,
    following, attn_out, hidden_out, g_vm, a_vm, o_vm, sems, out_sems, next_sem,
):
    pieces = (h0, h1, h2, h3)
    rows = own.shape[0]
    cols = g_vm.shape[3]
    copies = []
    for k in range(4):
        cp = pltpu.make_async_copy(g_hbm.at[:, scal[3 + k]], g_vm.at[k], sems.at[k])
        cp.start()
        copies.append(cp)
    accs = [None] * 4
    for k in range(4):
        copies[k].wait()
        hk = pieces[k][...]
        for c in range(4):
            term = jnp.dot(hk, g_vm[k, c], preferred_element_type=jnp.float32)
            accs[c] = term if accs[c] is None else accs[c] + term
    attn = jnp.concatenate(accs, axis=1)
    hid = (own[...].astype(jnp.float32) + attn).astype(jnp.bfloat16)
    live = jnp.broadcast_to(scal[1], attn.shape) != 0
    a_vm[...] = jnp.where(live, attn, 0.0).astype(jnp.bfloat16)
    o_vm[...] = jnp.where(live, hid.astype(jnp.float32), 0.0).astype(jnp.bfloat16)
    following[...] = hid

    @pl.when(scal[7] != 0)
    def _():
        nxt = pl.multiple_of(scal[8], rows)
        cp = pltpu.make_async_copy(hid_in.at[pl.ds(nxt, rows), :], following, next_sem)
        cp.start()
        cp.wait()

    @pl.when(scal[2] != 0)
    def _():
        row0 = pl.multiple_of(scal[0], rows)
        c1 = pltpu.make_async_copy(a_vm, attn_out.at[pl.ds(row0, rows), :], out_sems.at[0])
        c2 = pltpu.make_async_copy(o_vm, hidden_out.at[pl.ds(row0, rows), :], out_sems.at[1])
        c1.start()
        c2.start()
        c1.wait()
        c2.wait()


def project(scal, heads, own, hid_in, g, attn_buf, hid_buf):
    rows, part = own.shape
    vm = pl.BlockSpec(memory_space=pltpu.VMEM)
    hbm = pl.BlockSpec(memory_space=pl.ANY)
    depth, cols = g.shape[2], g.shape[3]
    return pl.pallas_call(
        project_kernel,
        out_shape=(
            jax.ShapeDtypeStruct((rows, part), jnp.bfloat16),
            jax.ShapeDtypeStruct(attn_buf.shape, jnp.bfloat16),
            jax.ShapeDtypeStruct(hid_buf.shape, jnp.bfloat16),
        ),
        in_specs=[pl.BlockSpec(memory_space=pltpu.SMEM)] + [vm] * 5 + [hbm] * 4,
        out_specs=(vm, hbm, hbm),
        input_output_aliases={8: 1, 9: 2},
        scratch_shapes=[
            pltpu.VMEM((4, 4, depth, cols), jnp.bfloat16),
            pltpu.VMEM((rows, part), jnp.bfloat16),
            pltpu.VMEM((rows, part), jnp.bfloat16),
            pltpu.SemaphoreType.DMA((4,)),
            pltpu.SemaphoreType.DMA((2,)),
            pltpu.SemaphoreType.DMA,
        ],
        compiler_params=pltpu.CompilerParams(vmem_limit_bytes=40 * 2**20),
        cost_estimate=pl.CostEstimate(
            flops=2 * rows * 4 * depth * part, bytes_accessed=2 * 4 * depth * part, transcendentals=0
        ),
        name="project",
    )(scal, *heads, own, hid_in, g, attn_buf, hid_buf)


def shards(hidden_in, kv_cache, norm_gain, w_query, w_keyval, w_out, stretch_count, prefix_len):
    section_idx = lax.axis_index("section")
    section_total = lax.axis_size("section")
    tensor_idx = lax.axis_index("tensor")
    tensor_total = lax.axis_size("tensor")
    dp_total = lax.axis_size("dp")
    rows_all, part = hidden_in.shape
    block = w_query.shape[1]
    w_local = jnp.concatenate([w_query[0], w_keyval[0, :, 0], w_keyval[0, :, 1]], axis=1)
    w_in = lax.all_gather(w_local, "dp", axis=0, tiled=True)
    per = dp_total // tensor_total
    pairs = []
    for d in range(dp_total):
        for t in range(tensor_total):
            d2, t2 = (d % per) * tensor_total + t, d // per
            pairs.append((d * tensor_total + t, d2 * tensor_total + t2))
    g_local = lax.ppermute(w_out[0], ("dp", "tensor"), pairs)
    g = lax.all_gather(g_local, "dp", axis=0, tiled=False)
    g = g.reshape(per, tensor_total, g.shape[1], g.shape[2])

    order = [(tensor_idx - k) % tensor_total for k in range(tensor_total)]
    gain = norm_gain[0].reshape(tensor_total, 1, part)
    gain = jnp.concatenate([lax.dynamic_slice_in_dim(gain, o, 1, 0) for o in order], axis=0)
    prefix = prefix_len[0]
    live_count = stretch_count[0]
    half = HEAD_DIM // 2
    inv_freq = theta_base ** (-(jnp.arange(half, dtype=jnp.float32) * 2.0 / HEAD_DIM))
    positions = prefix + jnp.arange(rows_all, dtype=jnp.int32)
    angles = positions.astype(jnp.float32)[:, None] * inv_freq[None, :]
    cos_t = jnp.cos(angles)
    sin_t = jnp.sin(angles)
    cos_t = jnp.concatenate([cos_t, cos_t], axis=1)
    sin_t = jnp.concatenate([-sin_t, sin_t], axis=1)
    kv = kv_cache[0, 0]

    kbuf = jnp.zeros((rows_all, HEAD_DIM), jnp.bfloat16)
    vbuf = jnp.zeros((rows_all, HEAD_DIM), jnp.bfloat16)
    attn_buf = jnp.zeros((rows_all, part), jnp.bfloat16)
    hid_buf = jnp.zeros((rows_all, part), jnp.bfloat16)
    rows = STRETCH // SUBS
    slot_total = rows_all // STRETCH
    tick_total = slot_total + section_total - 1
    owns = [hidden_in[i * rows : (i + 1) * rows] for i in range(SUBS)]
    is_last = (section_idx == section_total - 1).astype(jnp.int32)
    for tick in range(tick_total):
        slot = tick - section_idx
        valid = ((slot >= 0) & (slot < slot_total)).astype(jnp.int32)
        slot_safe = jnp.clip(slot, 0, slot_total - 1)
        live = (slot_safe < live_count).astype(jnp.int32)
        nxt_slot = min(tick + 1, slot_total - 1)
        for sub in range(SUBS):
            own = owns[sub]
            row0 = slot_safe * STRETCH + sub * rows
            scal = jnp.stack([row0, prefix] + order)
            pieces = spread(own, "tensor")
            heads, kbuf, vbuf = attend(scal, pieces, gain, cos_t, sin_t, kv, kbuf, vbuf, w_in)
            head_pieces = spread(heads, "tensor")
            scal2 = jnp.stack(
                [row0, live, valid] + order
                + [is_last, jnp.int32(nxt_slot * STRETCH + sub * rows)]
            )
            following, attn_buf, hid_buf = project(
                scal2, head_pieces, own, hidden_in, g, attn_buf, hid_buf
            )
            if tick + 1 < tick_total:
                owns[sub] = shift(following, "section", 1)
    return (attn_buf[None], hid_buf[None])


def solution(mesh):
    return jax.shard_map(
        shards,
        mesh=mesh,
        in_specs=(
            P("dp", "tensor"),
            P("section", "dp", None, None, "tensor"),
            P("section", None),
            P("section", "dp", "tensor"),
            P("section", "dp", None, "tensor"),
            P("section", "tensor", "dp"),
            P("dp"),
            P("dp"),
        ),
        out_specs=(P("section", "dp", "tensor"), P("section", "dp", "tensor")),
        check_vma=False,
    )
```

```python
import functools

import jax
import jax.numpy as jnp
from jax import lax
from jax.experimental import pallas as pl
from jax.experimental.pallas import tpu as pltpu
from jax.sharding import PartitionSpec as P

HEAD_DIM = 128
STRETCH = 128
SUBS = 1

theta_base = 1000000.0
eps_norm = 1e-06
masked_score = -1e30
score_scale = HEAD_DIM**-0.5 * 1.4426950408889634
VMEM_LIMIT = 36 * 2**20


def shift(value, axis, steps):
    count = lax.axis_size(axis)
    return lax.ppermute(value, axis, [(i, (i + steps) % count) for i in range(count)])


def spread(value, axis):
    return [value] + [shift(value, axis, k) for k in range(1, lax.axis_size(axis))]


def attend_kernel(
    tick, sub, scal, x0, x1, x2, x3, gain, cos_t, sin_t, kv, kin, vin, w,
    heads, kout, vout, q_vm, k_vm, v_vm, bias_vm, s_vm, p_vm, d_vm,
):
    pieces = (x0, x1, x2, x3)
    rows, part = x0.shape
    slots = kin.shape[0] // STRETCH
    slot = jnp.clip(tick - scal[0], 0, slots - 1)
    row0 = pl.multiple_of(slot * STRETCH + sub * rows, rows)
    prefix = scal[1]
    cap = kv.shape[1]
    new_rows = kin.shape[0]
    for j in range(3):
        k_vm[:cap, j * HEAD_DIM : (j + 1) * HEAD_DIM] = kv[0]
    v_vm[:cap, :] = kv[1]
    kept = lax.broadcasted_iota(jnp.int32, (rows, cap), 1) < prefix
    bias_vm[:, :cap] = jnp.where(kept, 0.0, masked_score)
    fresh = lax.broadcasted_iota(jnp.int32, (rows, new_rows), 1) <= (
        row0 + lax.broadcasted_iota(jnp.int32, (rows, new_rows), 0)
    )
    bias_vm[:, cap:] = jnp.where(fresh, 0.0, masked_score)
    kout[...] = kin[...]
    vout[...] = vin[...]
    total = None
    for k in range(4):
        xf = pieces[k][...].astype(jnp.float32)
        part_sum = jnp.sum(xf * xf, axis=1, keepdims=True)
        total = part_sum if total is None else total + part_sum
    scale = lax.rsqrt(total / (4 * part) + eps_norm)
    acc = None
    for k in range(4):
        normed = (pieces[k][...].astype(jnp.float32) * scale * gain[k]).astype(jnp.bfloat16)
        src = pl.multiple_of(scal[3 + k] * part, part)
        term = jnp.dot(normed, w[pl.ds(src, part), :], preferred_element_type=jnp.float32)
        acc = term if acc is None else acc + term
    cosv = cos_t[pl.ds(row0, rows), :]
    sinv = sin_t[pl.ds(row0, rows), :]
    n_heads = heads.shape[1] // HEAD_DIM

    def rot(v):
        return v * cosv + pltpu.roll(v, HEAD_DIM // 2, 1) * sinv

    for h in range(n_heads):
        qh = rot(acc[:, h * HEAD_DIM : (h + 1) * HEAD_DIM]) * score_scale
        hi = qh.astype(jnp.bfloat16)
        rem = qh - hi.astype(jnp.float32)
        mid = rem.astype(jnp.bfloat16)
        low = (rem - mid.astype(jnp.float32)).astype(jnp.bfloat16)
        q_vm[h * rows : (h + 1) * rows, :HEAD_DIM] = hi
        q_vm[h * rows : (h + 1) * rows, HEAD_DIM : 2 * HEAD_DIM] = mid
        q_vm[h * rows : (h + 1) * rows, 2 * HEAD_DIM :] = low
    base = n_heads * HEAD_DIM
    kout[pl.ds(row0, rows), :] = rot(acc[:, base : base + HEAD_DIM]).astype(jnp.bfloat16)
    vout[pl.ds(row0, rows), :] = acc[:, base + HEAD_DIM :].astype(jnp.bfloat16)
    for j in range(3):
        k_vm[cap:, j * HEAD_DIM : (j + 1) * HEAD_DIM] = kout[...]
    v_vm[cap:, :] = vout[...]
    s_vm[...] = lax.dot_general(
        q_vm[...], k_vm[...], (((1,), (1,)), ((), ())), preferred_element_type=jnp.float32
    )
    step = rows

    def softmax(i, carry):
        r = pl.multiple_of(i * step, step)
        b = pl.multiple_of(lax.rem(i * step, rows), step)
        s = s_vm[pl.ds(r, step), :] + bias_vm[pl.ds(b, step), :]
        e = jnp.exp2(s - jnp.max(s, axis=1, keepdims=True))
        d_vm[pl.ds(r, step), :] = jnp.broadcast_to(
            1.0 / jnp.sum(e, axis=1, keepdims=True), (step, HEAD_DIM)
        )
        p_vm[pl.ds(r, step), :] = e.astype(jnp.bfloat16)
        return carry

    lax.fori_loop(0, n_heads * rows // step, softmax, 0, unroll=True)
    out = jnp.dot(p_vm[...], v_vm[...], preferred_element_type=jnp.float32) * d_vm[...]
    for h in range(n_heads):
        heads[:, h * HEAD_DIM : (h + 1) * HEAD_DIM] = out[h * rows : (h + 1) * rows].astype(
            jnp.bfloat16
        )


def attend(tick, sub, scal, pieces, gain, cos_t, sin_t, kv, kin, vin, w):
    rows, part = pieces[0].shape
    cols = w.shape[1]
    n_heads = cols // HEAD_DIM - 2
    keys = kv.shape[1] + kin.shape[0]
    vm = pl.BlockSpec(memory_space=pltpu.VMEM)
    flops = 2 * rows * (4 * part * cols + 4 * n_heads * HEAD_DIM * keys)
    return pl.pallas_call(
        functools.partial(attend_kernel, tick, sub),
        out_shape=(
            jax.ShapeDtypeStruct((rows, n_heads * HEAD_DIM), jnp.bfloat16),
            jax.ShapeDtypeStruct(kin.shape, jnp.bfloat16),
            jax.ShapeDtypeStruct(vin.shape, jnp.bfloat16),
        ),
        in_specs=[pl.BlockSpec(memory_space=pltpu.SMEM)]
        + [vm] * 11,
        out_specs=(vm, vm, vm),
        scratch_shapes=[
            pltpu.VMEM((n_heads * rows, 3 * HEAD_DIM), jnp.bfloat16),
            pltpu.VMEM((keys, 3 * HEAD_DIM), jnp.bfloat16),
            pltpu.VMEM((keys, HEAD_DIM), jnp.bfloat16),
            pltpu.VMEM((rows, keys), jnp.float32),
            pltpu.VMEM((n_heads * rows, keys), jnp.float32),
            pltpu.VMEM((n_heads * rows, keys), jnp.bfloat16),
            pltpu.VMEM((n_heads * rows, HEAD_DIM), jnp.float32),
        ],
        compiler_params=pltpu.CompilerParams(vmem_limit_bytes=VMEM_LIMIT),
        cost_estimate=pl.CostEstimate(
            flops=flops, bytes_accessed=2 * 4 * part * cols, transcendentals=0
        ),
        name="attend",
    )(scal, *pieces, gain, cos_t, sin_t, kv, kin, vin, w)


def project_kernel(
    tick, sub, sections, scal, h0, h1, h2, h3, own, g, hid_in, attn_in, hidden_in,
    following, attn_out, hidden_out, a_vm, o_vm, out_sems, next_sem,
):
    pieces = (h0, h1, h2, h3)
    rows = own.shape[0]
    depth = h0.shape[1]
    slots = hid_in.shape[0] // STRETCH
    slot = tick - scal[0]
    valid = (slot >= 0) & (slot < slots)
    alive = (slot < scal[2]).astype(jnp.int32)
    attn = None
    for k in range(4):
        src = pl.multiple_of(scal[3 + k] * depth, depth)
        term = jnp.dot(
            pieces[k][...], g[pl.ds(src, depth), :], preferred_element_type=jnp.float32
        )
        attn = term if attn is None else attn + term
    hid = (own[...].astype(jnp.float32) + attn).astype(jnp.bfloat16)
    live = jnp.broadcast_to(alive, attn.shape) != 0
    a_vm[...] = jnp.where(live, attn, 0.0).astype(jnp.bfloat16)
    o_vm[...] = jnp.where(live, hid.astype(jnp.float32), 0.0).astype(jnp.bfloat16)
    following[...] = hid

    if tick + 1 < slots:

        @pl.when(scal[0] == sections - 1)
        def _():
            nxt = (tick + 1) * STRETCH + sub * rows
            cp = pltpu.make_async_copy(hid_in.at[pl.ds(nxt, rows), :], following, next_sem)
            cp.start()
            cp.wait()

    @pl.when(valid)
    def _():
        row0 = pl.multiple_of(jnp.clip(slot, 0, slots - 1) * STRETCH + sub * rows, rows)
        c1 = pltpu.make_async_copy(a_vm, attn_out.at[pl.ds(row0, rows), :], out_sems.at[0])
        c2 = pltpu.make_async_copy(o_vm, hidden_out.at[pl.ds(row0, rows), :], out_sems.at[1])
        c1.start()
        c2.start()
        c1.wait()
        c2.wait()


def project(tick, sub, sections, scal, heads, own, hid_in, g, attn_buf, hid_buf):
    rows, part = own.shape
    vm = pl.BlockSpec(memory_space=pltpu.VMEM)
    hbm = pl.BlockSpec(memory_space=pltpu.HBM)
    depth = g.shape[0] // 4
    return pl.pallas_call(
        functools.partial(project_kernel, tick, sub, sections),
        out_shape=(
            jax.ShapeDtypeStruct((rows, part), jnp.bfloat16),
            jax.ShapeDtypeStruct(attn_buf.shape, jnp.bfloat16),
            jax.ShapeDtypeStruct(hid_buf.shape, jnp.bfloat16),
        ),
        in_specs=[pl.BlockSpec(memory_space=pltpu.SMEM)] + [vm] * 6 + [hbm] * 3,
        out_specs=(vm, hbm, hbm),
        input_output_aliases={8: 1, 9: 2},
        scratch_shapes=[
            pltpu.VMEM((rows, part), jnp.bfloat16),
            pltpu.VMEM((rows, part), jnp.bfloat16),
            pltpu.SemaphoreType.DMA((2,)),
            pltpu.SemaphoreType.DMA,
        ],
        compiler_params=pltpu.CompilerParams(vmem_limit_bytes=VMEM_LIMIT),
        cost_estimate=pl.CostEstimate(
            flops=2 * rows * 4 * depth * part, bytes_accessed=2 * 4 * depth * part, transcendentals=0
        ),
        name="project",
    )(scal, *heads, own, g, hid_in, attn_buf, hid_buf)


def shards(hidden_in, kv_cache, norm_gain, w_query, w_keyval, w_out, stretch_count, prefix_len):
    section_idx = lax.axis_index("section")
    section_total = lax.axis_size("section")
    tensor_idx = lax.axis_index("tensor")
    tensor_total = lax.axis_size("tensor")
    dp_total = lax.axis_size("dp")
    rows_all, part = hidden_in.shape
    dp_idx = lax.axis_index("dp")
    per = dp_total // tensor_total
    block = w_query.shape[1]
    w_local = jnp.concatenate([w_query[0], w_keyval[0, :, 0], w_keyval[0, :, 1]], axis=1)
    depth, narrow = w_out.shape[1:]
    piece = depth // per
    received = []
    for k in range(per):
        pairs = []
        for d in range(dp_total):
            for t in range(tensor_total):
                p = (d % per + k) % per
                pairs.append((d * tensor_total + t, (t * per + p) * tensor_total + d // per))
        cut = lax.dynamic_slice_in_dim(w_out[0], (dp_idx % per + k) % per * piece, piece, 0)
        received.append(lax.ppermute(cut, ("dp", "tensor"), pairs))
    received = jnp.stack(received)
    g_local = jnp.concatenate(
        [
            lax.dynamic_index_in_dim(received, (dp_idx % per - c) % per, 0, keepdims=False)
            for c in range(per)
        ],
        axis=1,
    )

    w_in = lax.all_gather(w_local, "dp", axis=0, tiled=True)
    g_local, w_local = lax.optimization_barrier((g_local, w_local))
    g = lax.all_gather(g_local, "dp", axis=0, tiled=True)

    order = [(tensor_idx - k) % tensor_total for k in range(tensor_total)]
    gain = norm_gain[0].reshape(tensor_total, 1, part)
    gain = jnp.concatenate([lax.dynamic_slice_in_dim(gain, o, 1, 0) for o in order], axis=0)
    prefix = prefix_len[0]
    meta = jnp.stack([section_idx, prefix, stretch_count[0]] + order)
    half = HEAD_DIM // 2
    inv_freq = theta_base ** (-(jnp.arange(half, dtype=jnp.float32) * 2.0 / HEAD_DIM))
    positions = prefix + jnp.arange(rows_all, dtype=jnp.int32)
    angles = positions.astype(jnp.float32)[:, None] * inv_freq[None, :]
    cos_t = jnp.cos(angles)
    sin_t = jnp.sin(angles)
    cos_t = jnp.concatenate([cos_t, cos_t], axis=1)
    sin_t = jnp.concatenate([-sin_t, sin_t], axis=1)
    kv = kv_cache[0, 0]

    kbuf = jnp.zeros((rows_all, HEAD_DIM), jnp.bfloat16)
    vbuf = jnp.zeros((rows_all, HEAD_DIM), jnp.bfloat16)
    attn_buf = jnp.zeros((rows_all, part), jnp.bfloat16)
    hid_buf = jnp.zeros((rows_all, part), jnp.bfloat16)
    rows = STRETCH // SUBS
    slot_total = rows_all // STRETCH
    tick_total = slot_total + section_total - 1
    owns = [hidden_in[i * rows : (i + 1) * rows] for i in range(SUBS)]
    for tick in range(tick_total):
        for sub in range(SUBS):
            own = owns[sub]
            pieces = spread(own, "tensor")
            heads, kbuf, vbuf = attend(
                tick, sub, meta, pieces, gain, cos_t, sin_t, kv, kbuf, vbuf, w_in
            )
            head_pieces = spread(heads, "tensor")
            following, attn_buf, hid_buf = project(
                tick, sub, section_total, meta, head_pieces, own, hidden_in, g, attn_buf, hid_buf
            )
            if tick + 1 < tick_total:
                owns[sub] = shift(following, "section", 1)
    return (attn_buf[None], hid_buf[None])


def solution(mesh):
    return jax.shard_map(
        shards,
        mesh=mesh,
        in_specs=(
            P("dp", "tensor"),
            P("section", "dp", None, None, "tensor"),
            P("section", None),
            P("section", "dp", "tensor"),
            P("section", "dp", None, "tensor"),
            P("section", "tensor", "dp"),
            P("dp"),
            P("dp"),
        ),
        out_specs=(P("section", "dp", "tensor"), P("section", "dp", "tensor")),
        check_vma=False,
    )
```

```python
import functools

import jax
import jax.numpy as jnp
from jax import lax
from jax.experimental import pallas as pl
from jax.experimental.pallas import tpu as pltpu
from jax.sharding import PartitionSpec as P

HEAD_DIM = 128
STRETCH = 128
SUBS = 2

theta_base = 1000000.0
eps_norm = 1e-06
masked_score = -1e30
score_scale = HEAD_DIM**-0.5 * 1.4426950408889634
VMEM_LIMIT = 36 * 2**20


def shift(value, axis, steps):
    count = lax.axis_size(axis)
    return lax.ppermute(value, axis, [(i, (i + steps) % count) for i in range(count)])


def spread(value, axis):
    return [value] + [shift(value, axis, k) for k in range(1, lax.axis_size(axis))]


def attend_kernel(
    tick, sub, scal, x0, x1, x2, x3, gain, cos_t, sin_t, kv, kin, vin, w,
    heads, kout, vout, q_vm, k_vm, v_vm, bias_vm, s_vm, p_vm, d_vm,
):
    pieces = (x0, x1, x2, x3)
    rows, part = x0.shape
    slots = kin.shape[0] // STRETCH
    slot = jnp.clip(tick - scal[0], 0, slots - 1)
    row0 = pl.multiple_of(slot * STRETCH + sub * rows, rows)
    prefix = scal[1]
    cap = kv.shape[1]
    new_rows = kin.shape[0]
    for j in range(3):
        k_vm[:cap, j * HEAD_DIM : (j + 1) * HEAD_DIM] = kv[0]
    v_vm[:cap, :] = kv[1]
    kept = lax.broadcasted_iota(jnp.int32, (rows, cap), 1) < prefix
    bias_vm[:, :cap] = jnp.where(kept, 0.0, masked_score)
    fresh = lax.broadcasted_iota(jnp.int32, (rows, new_rows), 1) <= (
        row0 + lax.broadcasted_iota(jnp.int32, (rows, new_rows), 0)
    )
    bias_vm[:, cap:] = jnp.where(fresh, 0.0, masked_score)
    kout[...] = kin[...]
    vout[...] = vin[...]
    total = None
    for k in range(4):
        xf = pieces[k][...].astype(jnp.float32)
        part_sum = jnp.sum(xf * xf, axis=1, keepdims=True)
        total = part_sum if total is None else total + part_sum
    scale = lax.rsqrt(total / (4 * part) + eps_norm)
    acc = None
    for k in range(4):
        normed = (pieces[k][...].astype(jnp.float32) * scale * gain[k]).astype(jnp.bfloat16)
        src = pl.multiple_of(scal[3 + k] * part, part)
        term = jnp.dot(normed, w[pl.ds(src, part), :], preferred_element_type=jnp.float32)
        acc = term if acc is None else acc + term
    cosv = cos_t[pl.ds(row0, rows), :]
    sinv = sin_t[pl.ds(row0, rows), :]
    n_heads = heads.shape[1] // HEAD_DIM

    def rot(v):
        return v * cosv + pltpu.roll(v, HEAD_DIM // 2, 1) * sinv

    for h in range(n_heads):
        qh = rot(acc[:, h * HEAD_DIM : (h + 1) * HEAD_DIM]) * score_scale
        hi = qh.astype(jnp.bfloat16)
        rem = qh - hi.astype(jnp.float32)
        mid = rem.astype(jnp.bfloat16)
        low = (rem - mid.astype(jnp.float32)).astype(jnp.bfloat16)
        q_vm[h * rows : (h + 1) * rows, :HEAD_DIM] = hi
        q_vm[h * rows : (h + 1) * rows, HEAD_DIM : 2 * HEAD_DIM] = mid
        q_vm[h * rows : (h + 1) * rows, 2 * HEAD_DIM :] = low
    base = n_heads * HEAD_DIM
    kout[pl.ds(row0, rows), :] = rot(acc[:, base : base + HEAD_DIM]).astype(jnp.bfloat16)
    vout[pl.ds(row0, rows), :] = acc[:, base + HEAD_DIM :].astype(jnp.bfloat16)
    for j in range(3):
        k_vm[cap:, j * HEAD_DIM : (j + 1) * HEAD_DIM] = kout[...]
    v_vm[cap:, :] = vout[...]
    s_vm[...] = lax.dot_general(
        q_vm[...], k_vm[...], (((1,), (1,)), ((), ())), preferred_element_type=jnp.float32
    )
    step = rows

    def softmax(i, carry):
        r = pl.multiple_of(i * step, step)
        b = pl.multiple_of(lax.rem(i * step, rows), step)
        s = s_vm[pl.ds(r, step), :] + bias_vm[pl.ds(b, step), :]
        e = jnp.exp2(s - jnp.max(s, axis=1, keepdims=True))
        d_vm[pl.ds(r, step), :] = jnp.broadcast_to(
            1.0 / jnp.sum(e, axis=1, keepdims=True), (step, HEAD_DIM)
        )
        p_vm[pl.ds(r, step), :] = e.astype(jnp.bfloat16)
        return carry

    lax.fori_loop(0, n_heads * rows // step, softmax, 0, unroll=True)
    out = jnp.dot(p_vm[...], v_vm[...], preferred_element_type=jnp.float32) * d_vm[...]
    for h in range(n_heads):
        heads[:, h * HEAD_DIM : (h + 1) * HEAD_DIM] = out[h * rows : (h + 1) * rows].astype(
            jnp.bfloat16
        )


def attend(tick, sub, scal, pieces, gain, cos_t, sin_t, kv, kin, vin, w):
    rows, part = pieces[0].shape
    cols = w.shape[1]
    n_heads = cols // HEAD_DIM - 2
    keys = kv.shape[1] + kin.shape[0]
    vm = pl.BlockSpec(memory_space=pltpu.VMEM)
    flops = 2 * rows * (4 * part * cols + 4 * n_heads * HEAD_DIM * keys)
    return pl.pallas_call(
        functools.partial(attend_kernel, tick, sub),
        out_shape=(
            jax.ShapeDtypeStruct((rows, n_heads * HEAD_DIM), jnp.bfloat16),
            jax.ShapeDtypeStruct(kin.shape, jnp.bfloat16),
            jax.ShapeDtypeStruct(vin.shape, jnp.bfloat16),
        ),
        in_specs=[pl.BlockSpec(memory_space=pltpu.SMEM)]
        + [vm] * 11,
        out_specs=(vm, vm, vm),
        scratch_shapes=[
            pltpu.VMEM((n_heads * rows, 3 * HEAD_DIM), jnp.bfloat16),
            pltpu.VMEM((keys, 3 * HEAD_DIM), jnp.bfloat16),
            pltpu.VMEM((keys, HEAD_DIM), jnp.bfloat16),
            pltpu.VMEM((rows, keys), jnp.float32),
            pltpu.VMEM((n_heads * rows, keys), jnp.float32),
            pltpu.VMEM((n_heads * rows, keys), jnp.bfloat16),
            pltpu.VMEM((n_heads * rows, HEAD_DIM), jnp.float32),
        ],
        compiler_params=pltpu.CompilerParams(vmem_limit_bytes=VMEM_LIMIT),
        cost_estimate=pl.CostEstimate(
            flops=flops, bytes_accessed=2 * 4 * part * cols, transcendentals=0
        ),
        name="attend",
    )(scal, *pieces, gain, cos_t, sin_t, kv, kin, vin, w)


def project_kernel(
    tick, sub, sections, scal, h0, h1, h2, h3, own, g, hid_in, attn_in, hidden_in,
    following, attn_out, hidden_out, a_vm, o_vm, out_sems, next_sem,
):
    pieces = (h0, h1, h2, h3)
    rows = own.shape[0]
    depth = h0.shape[1]
    slots = hid_in.shape[0] // STRETCH
    slot = tick - scal[0]
    valid = (slot >= 0) & (slot < slots)
    alive = (slot < scal[2]).astype(jnp.int32)
    attn = None
    for k in range(4):
        src = pl.multiple_of(scal[3 + k] * depth, depth)
        term = jnp.dot(
            pieces[k][...], g[pl.ds(src, depth), :], preferred_element_type=jnp.float32
        )
        attn = term if attn is None else attn + term
    hid = (own[...].astype(jnp.float32) + attn).astype(jnp.bfloat16)
    live = jnp.broadcast_to(alive, attn.shape) != 0
    a_vm[...] = jnp.where(live, attn, 0.0).astype(jnp.bfloat16)
    o_vm[...] = jnp.where(live, hid.astype(jnp.float32), 0.0).astype(jnp.bfloat16)
    following[...] = hid

    if tick + 1 < slots:

        @pl.when(scal[0] == sections - 1)
        def _():
            nxt = (tick + 1) * STRETCH + sub * rows
            cp = pltpu.make_async_copy(hid_in.at[pl.ds(nxt, rows), :], following, next_sem)
            cp.start()
            cp.wait()

    @pl.when(valid)
    def _():
        row0 = pl.multiple_of(jnp.clip(slot, 0, slots - 1) * STRETCH + sub * rows, rows)
        c1 = pltpu.make_async_copy(a_vm, attn_out.at[pl.ds(row0, rows), :], out_sems.at[0])
        c2 = pltpu.make_async_copy(o_vm, hidden_out.at[pl.ds(row0, rows), :], out_sems.at[1])
        c1.start()
        c2.start()
        c1.wait()
        c2.wait()


def project(tick, sub, sections, scal, heads, own, hid_in, g, attn_buf, hid_buf):
    rows, part = own.shape
    vm = pl.BlockSpec(memory_space=pltpu.VMEM)
    hbm = pl.BlockSpec(memory_space=pltpu.HBM)
    depth = g.shape[0] // 4
    return pl.pallas_call(
        functools.partial(project_kernel, tick, sub, sections),
        out_shape=(
            jax.ShapeDtypeStruct((rows, part), jnp.bfloat16),
            jax.ShapeDtypeStruct(attn_buf.shape, jnp.bfloat16),
            jax.ShapeDtypeStruct(hid_buf.shape, jnp.bfloat16),
        ),
        in_specs=[pl.BlockSpec(memory_space=pltpu.SMEM)] + [vm] * 6 + [hbm] * 3,
        out_specs=(vm, hbm, hbm),
        input_output_aliases={8: 1, 9: 2},
        scratch_shapes=[
            pltpu.VMEM((rows, part), jnp.bfloat16),
            pltpu.VMEM((rows, part), jnp.bfloat16),
            pltpu.SemaphoreType.DMA((2,)),
            pltpu.SemaphoreType.DMA,
        ],
        compiler_params=pltpu.CompilerParams(vmem_limit_bytes=VMEM_LIMIT),
        cost_estimate=pl.CostEstimate(
            flops=2 * rows * 4 * depth * part, bytes_accessed=2 * 4 * depth * part, transcendentals=0
        ),
        name="project",
    )(scal, *heads, own, g, hid_in, attn_buf, hid_buf)


def shards(hidden_in, kv_cache, norm_gain, w_query, w_keyval, w_out, stretch_count, prefix_len):
    section_idx = lax.axis_index("section")
    section_total = lax.axis_size("section")
    tensor_idx = lax.axis_index("tensor")
    tensor_total = lax.axis_size("tensor")
    dp_total = lax.axis_size("dp")
    rows_all, part = hidden_in.shape
    dp_idx = lax.axis_index("dp")
    per = dp_total // tensor_total
    block = w_query.shape[1]
    w_local = jnp.concatenate([w_query[0], w_keyval[0, :, 0], w_keyval[0, :, 1]], axis=1)
    depth, narrow = w_out.shape[1:]
    piece = depth // per
    received = []
    for k in range(per):
        pairs = []
        for d in range(dp_total):
            for t in range(tensor_total):
                p = (d % per + k) % per
                pairs.append((d * tensor_total + t, (t * per + p) * tensor_total + d // per))
        cut = lax.dynamic_slice_in_dim(w_out[0], (dp_idx % per + k) % per * piece, piece, 0)
        received.append(lax.ppermute(cut, ("dp", "tensor"), pairs))
    received = jnp.stack(received)
    g_local = jnp.concatenate(
        [
            lax.dynamic_index_in_dim(received, (dp_idx % per - c) % per, 0, keepdims=False)
            for c in range(per)
        ],
        axis=1,
    )

    w_in = lax.all_gather(w_local, "dp", axis=0, tiled=True)
    g_local, w_local = lax.optimization_barrier((g_local, w_local))
    g = lax.all_gather(g_local, "dp", axis=0, tiled=True)

    order = [(tensor_idx - k) % tensor_total for k in range(tensor_total)]
    gain = norm_gain[0].reshape(tensor_total, 1, part)
    gain = jnp.concatenate([lax.dynamic_slice_in_dim(gain, o, 1, 0) for o in order], axis=0)
    prefix = prefix_len[0]
    meta = jnp.stack([section_idx, prefix, stretch_count[0]] + order)
    half = HEAD_DIM // 2
    inv_freq = theta_base ** (-(jnp.arange(half, dtype=jnp.float32) * 2.0 / HEAD_DIM))
    positions = prefix + jnp.arange(rows_all, dtype=jnp.int32)
    angles = positions.astype(jnp.float32)[:, None] * inv_freq[None, :]
    cos_t = jnp.cos(angles)
    sin_t = jnp.sin(angles)
    cos_t = jnp.concatenate([cos_t, cos_t], axis=1)
    sin_t = jnp.concatenate([-sin_t, sin_t], axis=1)
    kv = kv_cache[0, 0]

    kbuf = jnp.zeros((rows_all, HEAD_DIM), jnp.bfloat16)
    vbuf = jnp.zeros((rows_all, HEAD_DIM), jnp.bfloat16)
    attn_buf = jnp.zeros((rows_all, part), jnp.bfloat16)
    hid_buf = jnp.zeros((rows_all, part), jnp.bfloat16)
    rows = STRETCH // SUBS
    slot_total = rows_all // STRETCH
    tick_total = slot_total + section_total - 1
    owns = [hidden_in[i * rows : (i + 1) * rows] for i in range(SUBS)]
    for tick in range(tick_total):
        for sub in range(SUBS):
            own = owns[sub]
            pieces = spread(own, "tensor")
            heads, kbuf, vbuf = attend(
                tick, sub, meta, pieces, gain, cos_t, sin_t, kv, kbuf, vbuf, w_in
            )
            head_pieces = spread(heads, "tensor")
            following, attn_buf, hid_buf = project(
                tick, sub, section_total, meta, head_pieces, own, hidden_in, g, attn_buf, hid_buf
            )
            if tick + 1 < tick_total:
                owns[sub] = shift(following, "section", 1)
    return (attn_buf[None], hid_buf[None])


def solution(mesh):
    return jax.shard_map(
        shards,
        mesh=mesh,
        in_specs=(
            P("dp", "tensor"),
            P("section", "dp", None, None, "tensor"),
            P("section", None),
            P("section", "dp", "tensor"),
            P("section", "dp", None, "tensor"),
            P("section", "tensor", "dp"),
            P("dp"),
            P("dp"),
        ),
        out_specs=(P("section", "dp", "tensor"), P("section", "dp", "tensor")),
        check_vma=False,
    )
```

```python
import functools

import jax
import jax.numpy as jnp
from jax import lax
from jax.experimental import pallas as pl
from jax.experimental.pallas import tpu as pltpu
from jax.sharding import PartitionSpec as P

HEAD_DIM = 128
STRETCH = 128
SUBS = 2

theta_base = 1000000.0
eps_norm = 1e-06
masked_score = -1e30
score_scale = HEAD_DIM**-0.5 * 1.4426950408889634
VMEM_LIMIT = 36 * 2**20


def shift(value, axis, steps):
    count = lax.axis_size(axis)
    return lax.ppermute(value, axis, [(i, (i + steps) % count) for i in range(count)])


def spread(value, axis):
    return [value] + [shift(value, axis, k) for k in range(1, lax.axis_size(axis))]


def attend_kernel(
    tick, sub, scal, x0, x1, x2, x3, gain, cos_t, sin_t, kv, kin, vin, w,
    heads, kout, vout, q_vm, k_vm, v_vm, bias_vm, s_vm, p_vm, d_vm,
):
    pieces = (x0, x1, x2, x3)
    rows, part = x0.shape
    slots = kin.shape[0] // STRETCH
    slot = jnp.clip(tick - scal[0], 0, slots - 1)
    row0 = pl.multiple_of(slot * STRETCH + sub * rows, rows)
    prefix = scal[1]
    cap = kv.shape[1]
    new_rows = kin.shape[0]
    for j in range(3):
        k_vm[:cap, j * HEAD_DIM : (j + 1) * HEAD_DIM] = kv[0]
    v_vm[:cap, :] = kv[1]
    kept = lax.broadcasted_iota(jnp.int32, (rows, cap), 1) < prefix
    bias_vm[:, :cap] = jnp.where(kept, 0.0, masked_score)
    fresh = lax.broadcasted_iota(jnp.int32, (rows, new_rows), 1) <= (
        row0 + lax.broadcasted_iota(jnp.int32, (rows, new_rows), 0)
    )
    bias_vm[:, cap:] = jnp.where(fresh, 0.0, masked_score)
    kout[...] = kin[...]
    vout[...] = vin[...]
    total = None
    for k in range(4):
        xf = pieces[k][...].astype(jnp.float32)
        part_sum = jnp.sum(xf * xf, axis=1, keepdims=True)
        total = part_sum if total is None else total + part_sum
    scale = lax.rsqrt(total / (4 * part) + eps_norm)
    acc = None
    for k in range(4):
        normed = (pieces[k][...].astype(jnp.float32) * scale * gain[k]).astype(jnp.bfloat16)
        src = pl.multiple_of(scal[3 + k] * part, part)
        term = jnp.dot(normed, w[pl.ds(src, part), :], preferred_element_type=jnp.float32)
        acc = term if acc is None else acc + term
    cosv = cos_t[pl.ds(row0, rows), :]
    sinv = sin_t[pl.ds(row0, rows), :]
    n_heads = heads.shape[1] // HEAD_DIM

    def rot(v):
        return v * cosv + pltpu.roll(v, HEAD_DIM // 2, 1) * sinv

    for h in range(n_heads):
        qh = rot(acc[:, h * HEAD_DIM : (h + 1) * HEAD_DIM]) * score_scale
        hi = qh.astype(jnp.bfloat16)
        rem = qh - hi.astype(jnp.float32)
        mid = rem.astype(jnp.bfloat16)
        low = (rem - mid.astype(jnp.float32)).astype(jnp.bfloat16)
        q_vm[h * rows : (h + 1) * rows, :HEAD_DIM] = hi
        q_vm[h * rows : (h + 1) * rows, HEAD_DIM : 2 * HEAD_DIM] = mid
        q_vm[h * rows : (h + 1) * rows, 2 * HEAD_DIM :] = low
    base = n_heads * HEAD_DIM
    kout[pl.ds(row0, rows), :] = rot(acc[:, base : base + HEAD_DIM]).astype(jnp.bfloat16)
    vout[pl.ds(row0, rows), :] = acc[:, base + HEAD_DIM :].astype(jnp.bfloat16)
    for j in range(3):
        k_vm[cap:, j * HEAD_DIM : (j + 1) * HEAD_DIM] = kout[...]
    v_vm[cap:, :] = vout[...]
    s_vm[...] = lax.dot_general(
        q_vm[...], k_vm[...], (((1,), (1,)), ((), ())), preferred_element_type=jnp.float32
    )
    step = rows

    def softmax(i, carry):
        r = pl.multiple_of(i * step, step)
        b = pl.multiple_of(lax.rem(i * step, rows), step)
        s = s_vm[pl.ds(r, step), :] + bias_vm[pl.ds(b, step), :]
        e = jnp.exp2(s - jnp.max(s, axis=1, keepdims=True))
        d_vm[pl.ds(r, step), :] = jnp.broadcast_to(
            1.0 / jnp.sum(e, axis=1, keepdims=True), (step, HEAD_DIM)
        )
        p_vm[pl.ds(r, step), :] = e.astype(jnp.bfloat16)
        return carry

    lax.fori_loop(0, n_heads * rows // step, softmax, 0, unroll=True)
    out = jnp.dot(p_vm[...], v_vm[...], preferred_element_type=jnp.float32) * d_vm[...]
    for h in range(n_heads):
        heads[:, h * HEAD_DIM : (h + 1) * HEAD_DIM] = out[h * rows : (h + 1) * rows].astype(
            jnp.bfloat16
        )


def attend(tick, sub, scal, pieces, gain, cos_t, sin_t, kv, kin, vin, w):
    rows, part = pieces[0].shape
    cols = w.shape[1]
    n_heads = cols // HEAD_DIM - 2
    keys = kv.shape[1] + kin.shape[0]
    vm = pl.BlockSpec(memory_space=pltpu.VMEM)
    flops = 2 * rows * (4 * part * cols + 4 * n_heads * HEAD_DIM * keys)
    return pl.pallas_call(
        functools.partial(attend_kernel, tick, sub),
        out_shape=(
            jax.ShapeDtypeStruct((rows, n_heads * HEAD_DIM), jnp.bfloat16),
            jax.ShapeDtypeStruct(kin.shape, jnp.bfloat16),
            jax.ShapeDtypeStruct(vin.shape, jnp.bfloat16),
        ),
        in_specs=[pl.BlockSpec(memory_space=pltpu.SMEM)]
        + [vm] * 11,
        out_specs=(vm, vm, vm),
        scratch_shapes=[
            pltpu.VMEM((n_heads * rows, 3 * HEAD_DIM), jnp.bfloat16),
            pltpu.VMEM((keys, 3 * HEAD_DIM), jnp.bfloat16),
            pltpu.VMEM((keys, HEAD_DIM), jnp.bfloat16),
            pltpu.VMEM((rows, keys), jnp.float32),
            pltpu.VMEM((n_heads * rows, keys), jnp.float32),
            pltpu.VMEM((n_heads * rows, keys), jnp.bfloat16),
            pltpu.VMEM((n_heads * rows, HEAD_DIM), jnp.float32),
        ],
        compiler_params=pltpu.CompilerParams(vmem_limit_bytes=VMEM_LIMIT),
        cost_estimate=pl.CostEstimate(
            flops=flops, bytes_accessed=2 * 4 * part * cols, transcendentals=0
        ),
        name="attend",
    )(scal, *pieces, gain, cos_t, sin_t, kv, kin, vin, w)


def project_kernel(
    tick, sub, sections, scal, h0, h1, h2, h3, own, g, hid_in, attn_in, hidden_in,
    following, attn_out, hidden_out, a_vm, o_vm, out_sems, next_sem,
):
    pieces = (h0, h1, h2, h3)
    rows = own.shape[0]
    depth = h0.shape[1]
    slots = hid_in.shape[0] // STRETCH
    slot = tick - scal[0]
    valid = (slot >= 0) & (slot < slots)
    alive = (slot < scal[2]).astype(jnp.int32)
    attn = None
    for k in range(4):
        src = pl.multiple_of(scal[3 + k] * depth, depth)
        term = jnp.dot(
            pieces[k][...], g[pl.ds(src, depth), :], preferred_element_type=jnp.float32
        )
        attn = term if attn is None else attn + term
    hid = (own[...].astype(jnp.float32) + attn).astype(jnp.bfloat16)
    live = jnp.broadcast_to(alive, attn.shape) != 0
    a_vm[...] = jnp.where(live, attn, 0.0).astype(jnp.bfloat16)
    o_vm[...] = jnp.where(live, hid.astype(jnp.float32), 0.0).astype(jnp.bfloat16)
    following[...] = hid

    if tick + 1 < slots:

        @pl.when(scal[0] == sections - 1)
        def _():
            nxt = (tick + 1) * STRETCH + sub * rows
            cp = pltpu.make_async_copy(hid_in.at[pl.ds(nxt, rows), :], following, next_sem)
            cp.start()
            cp.wait()

    @pl.when(valid)
    def _():
        row0 = pl.multiple_of(jnp.clip(slot, 0, slots - 1) * STRETCH + sub * rows, rows)
        c1 = pltpu.make_async_copy(a_vm, attn_out.at[pl.ds(row0, rows), :], out_sems.at[0])
        c2 = pltpu.make_async_copy(o_vm, hidden_out.at[pl.ds(row0, rows), :], out_sems.at[1])
        c1.start()
        c2.start()
        c1.wait()
        c2.wait()


def project(tick, sub, sections, scal, heads, own, hid_in, g, attn_buf, hid_buf):
    rows, part = own.shape
    vm = pl.BlockSpec(memory_space=pltpu.VMEM)
    hbm = pl.BlockSpec(memory_space=pltpu.HBM)
    depth = g.shape[0] // 4
    return pl.pallas_call(
        functools.partial(project_kernel, tick, sub, sections),
        out_shape=(
            jax.ShapeDtypeStruct((rows, part), jnp.bfloat16),
            jax.ShapeDtypeStruct(attn_buf.shape, jnp.bfloat16),
            jax.ShapeDtypeStruct(hid_buf.shape, jnp.bfloat16),
        ),
        in_specs=[pl.BlockSpec(memory_space=pltpu.SMEM)] + [vm] * 6 + [hbm] * 3,
        out_specs=(vm, hbm, hbm),
        input_output_aliases={8: 1, 9: 2},
        scratch_shapes=[
            pltpu.VMEM((rows, part), jnp.bfloat16),
            pltpu.VMEM((rows, part), jnp.bfloat16),
            pltpu.SemaphoreType.DMA((2,)),
            pltpu.SemaphoreType.DMA,
        ],
        compiler_params=pltpu.CompilerParams(vmem_limit_bytes=VMEM_LIMIT),
        cost_estimate=pl.CostEstimate(
            flops=2 * rows * 4 * depth * part, bytes_accessed=2 * 4 * depth * part, transcendentals=0
        ),
        name="project",
    )(scal, *heads, own, g, hid_in, attn_buf, hid_buf)


def shards(hidden_in, kv_cache, norm_gain, w_query, w_keyval, w_out, stretch_count, prefix_len):
    section_idx = lax.axis_index("section")
    section_total = lax.axis_size("section")
    tensor_idx = lax.axis_index("tensor")
    tensor_total = lax.axis_size("tensor")
    dp_total = lax.axis_size("dp")
    rows_all, part = hidden_in.shape
    dp_idx = lax.axis_index("dp")
    per = dp_total // tensor_total
    block = w_query.shape[1]
    depth, narrow = w_out.shape[1:]
    halves = depth // block
    wide = per // halves
    my_half = dp_idx // wide % halves
    received = []
    for k in range(halves):
        pairs = []
        for d in range(dp_total):
            for t in range(tensor_total):
                d2 = (t * halves + (d + k) % halves) * wide + d % per // halves
                pairs.append((d * tensor_total + t, d2 * tensor_total + d // per))
        cut = lax.dynamic_slice_in_dim(w_out[0], (dp_idx + k) % halves * block, block, 0)
        received.append(lax.ppermute(cut, ("dp", "tensor"), pairs))
    columns = []
    for c in range(halves):
        chosen = received[0]
        for k in range(1, halves):
            chosen = jnp.where((my_half - c) % halves == k, received[k], chosen)
        columns.append(chosen)
    w_local = jnp.concatenate(
        [w_query[0], w_keyval[0, :, 0], w_keyval[0, :, 1]] + columns, axis=1
    )
    w_all = lax.all_gather(w_local, "dp", axis=0, tiled=True)
    in_cols = w_local.shape[1] - halves * narrow
    w_in = w_all[:, :in_cols]

    order = [(tensor_idx - k) % tensor_total for k in range(tensor_total)]
    gain = norm_gain[0].reshape(tensor_total, 1, part)
    gain = jnp.concatenate([lax.dynamic_slice_in_dim(gain, o, 1, 0) for o in order], axis=0)
    prefix = prefix_len[0]
    meta = jnp.stack([section_idx, prefix, stretch_count[0]] + order)
    half = HEAD_DIM // 2
    inv_freq = theta_base ** (-(jnp.arange(half, dtype=jnp.float32) * 2.0 / HEAD_DIM))
    positions = prefix + jnp.arange(rows_all, dtype=jnp.int32)
    angles = positions.astype(jnp.float32)[:, None] * inv_freq[None, :]
    cos_t = jnp.cos(angles)
    sin_t = jnp.sin(angles)
    cos_t = jnp.concatenate([cos_t, cos_t], axis=1)
    sin_t = jnp.concatenate([-sin_t, sin_t], axis=1)
    kv = kv_cache[0, 0]

    kbuf = jnp.zeros((rows_all, HEAD_DIM), jnp.bfloat16)
    vbuf = jnp.zeros((rows_all, HEAD_DIM), jnp.bfloat16)
    attn_buf = jnp.zeros((rows_all, part), jnp.bfloat16)
    hid_buf = jnp.zeros((rows_all, part), jnp.bfloat16)
    rows = STRETCH // SUBS
    slot_total = rows_all // STRETCH
    tick_total = slot_total + section_total - 1
    owns = [hidden_in[i * rows : (i + 1) * rows] for i in range(SUBS)]
    for tick in range(tick_total):
        heads = []
        for sub in range(SUBS):
            pieces = spread(owns[sub], "tensor")
            mixed, kbuf, vbuf = attend(
                tick, sub, meta, pieces, gain, cos_t, sin_t, kv, kbuf, vbuf, w_in
            )
            heads.append(spread(mixed, "tensor"))
        if tick == 0:
            w_all, kbuf = lax.optimization_barrier((w_all, kbuf))
            g = w_all[:, in_cols:].reshape(
                tensor_total, halves, wide, block, halves * narrow
            )
            g = g.transpose(0, 1, 3, 2, 4).reshape(tensor_total * depth, per * narrow)
        for sub in range(SUBS):
            own = owns[sub]
            following, attn_buf, hid_buf = project(
                tick, sub, section_total, meta, heads[sub], own, hidden_in, g, attn_buf, hid_buf
            )
            if tick + 1 < tick_total:
                owns[sub] = shift(following, "section", 1)
    return (attn_buf[None], hid_buf[None])


def solution(mesh):
    return jax.shard_map(
        shards,
        mesh=mesh,
        in_specs=(
            P("dp", "tensor"),
            P("section", "dp", None, None, "tensor"),
            P("section", None),
            P("section", "dp", "tensor"),
            P("section", "dp", None, "tensor"),
            P("section", "tensor", "dp"),
            P("dp"),
            P("dp"),
        ),
        out_specs=(P("section", "dp", "tensor"), P("section", "dp", "tensor")),
        check_vma=False,
    )
```

```python
import functools

import jax
import jax.numpy as jnp
from jax import lax
from jax.experimental import pallas as pl
from jax.experimental.pallas import tpu as pltpu
from jax.sharding import PartitionSpec as P

HEAD_DIM = 128
STRETCH = 128
SUBS = 2

theta_base = 1000000.0
eps_norm = 1e-06
masked_score = -1e30
score_scale = HEAD_DIM**-0.5 * 1.4426950408889634
VMEM_LIMIT = 36 * 2**20


def shift(value, axis, steps):
    count = lax.axis_size(axis)
    return lax.ppermute(value, axis, [(i, (i + steps) % count) for i in range(count)])


def spread(value, axis):
    return [value] + [shift(value, axis, k) for k in range(1, lax.axis_size(axis))]


def attend_kernel(
    tick, sub, scal, x0, x1, x2, x3, gain, cos_t, sin_t, kv, kin, vin, w,
    heads, kout, vout, q_vm, k_vm, v_vm, bias_vm, s_vm, p_vm, d_vm,
):
    pieces = (x0, x1, x2, x3)
    rows, part = x0.shape
    slots = kin.shape[0] // STRETCH
    slot = jnp.clip(tick - scal[0], 0, slots - 1)
    row0 = pl.multiple_of(slot * STRETCH + sub * rows, rows)
    prefix = scal[1]
    cap = kv.shape[1]
    new_rows = kin.shape[0]
    for j in range(3):
        k_vm[:cap, j * HEAD_DIM : (j + 1) * HEAD_DIM] = kv[0]
    v_vm[:cap, :] = kv[1]
    kept = lax.broadcasted_iota(jnp.int32, (rows, cap), 1) < prefix
    bias_vm[:, :cap] = jnp.where(kept, 0.0, masked_score)
    fresh = lax.broadcasted_iota(jnp.int32, (rows, new_rows), 1) <= (
        row0 + lax.broadcasted_iota(jnp.int32, (rows, new_rows), 0)
    )
    bias_vm[:, cap:] = jnp.where(fresh, 0.0, masked_score)
    kout[...] = kin[...]
    vout[...] = vin[...]
    total = None
    for k in range(4):
        xf = pieces[k][...].astype(jnp.float32)
        part_sum = jnp.sum(xf * xf, axis=1, keepdims=True)
        total = part_sum if total is None else total + part_sum
    scale = lax.rsqrt(total / (4 * part) + eps_norm)
    acc = None
    for k in range(4):
        normed = (pieces[k][...].astype(jnp.float32) * scale * gain[k]).astype(jnp.bfloat16)
        src = pl.multiple_of(scal[3 + k] * part, part)
        term = jnp.dot(normed, w[pl.ds(src, part), :], preferred_element_type=jnp.float32)
        acc = term if acc is None else acc + term
    cosv = cos_t[pl.ds(row0, rows), :]
    sinv = sin_t[pl.ds(row0, rows), :]
    n_heads = heads.shape[1] // HEAD_DIM

    def rot(v):
        return v * cosv + pltpu.roll(v, HEAD_DIM // 2, 1) * sinv

    for h in range(n_heads):
        qh = rot(acc[:, h * HEAD_DIM : (h + 1) * HEAD_DIM]) * score_scale
        hi = qh.astype(jnp.bfloat16)
        rem = qh - hi.astype(jnp.float32)
        mid = rem.astype(jnp.bfloat16)
        low = (rem - mid.astype(jnp.float32)).astype(jnp.bfloat16)
        q_vm[h * rows : (h + 1) * rows, :HEAD_DIM] = hi
        q_vm[h * rows : (h + 1) * rows, HEAD_DIM : 2 * HEAD_DIM] = mid
        q_vm[h * rows : (h + 1) * rows, 2 * HEAD_DIM :] = low
    base = n_heads * HEAD_DIM
    kout[pl.ds(row0, rows), :] = rot(acc[:, base : base + HEAD_DIM]).astype(jnp.bfloat16)
    vout[pl.ds(row0, rows), :] = acc[:, base + HEAD_DIM :].astype(jnp.bfloat16)
    for j in range(3):
        k_vm[cap:, j * HEAD_DIM : (j + 1) * HEAD_DIM] = kout[...]
    v_vm[cap:, :] = vout[...]
    s_vm[...] = lax.dot_general(
        q_vm[...], k_vm[...], (((1,), (1,)), ((), ())), preferred_element_type=jnp.float32
    )
    step = rows

    def softmax(i, carry):
        r = pl.multiple_of(i * step, step)
        b = pl.multiple_of(lax.rem(i * step, rows), step)
        s = s_vm[pl.ds(r, step), :] + bias_vm[pl.ds(b, step), :]
        e = jnp.exp2(s - jnp.max(s, axis=1, keepdims=True))
        d_vm[pl.ds(r, step), :] = jnp.broadcast_to(
            1.0 / jnp.sum(e, axis=1, keepdims=True), (step, HEAD_DIM)
        )
        p_vm[pl.ds(r, step), :] = e.astype(jnp.bfloat16)
        return carry

    lax.fori_loop(0, n_heads * rows // step, softmax, 0, unroll=True)
    out = jnp.dot(p_vm[...], v_vm[...], preferred_element_type=jnp.float32) * d_vm[...]
    for h in range(n_heads):
        heads[:, h * HEAD_DIM : (h + 1) * HEAD_DIM] = out[h * rows : (h + 1) * rows].astype(
            jnp.bfloat16
        )


def attend(tick, sub, scal, pieces, gain, cos_t, sin_t, kv, kin, vin, w):
    rows, part = pieces[0].shape
    cols = w.shape[1]
    n_heads = cols // HEAD_DIM - 2
    keys = kv.shape[1] + kin.shape[0]
    vm = pl.BlockSpec(memory_space=pltpu.VMEM)
    flops = 2 * rows * (4 * part * cols + 4 * n_heads * HEAD_DIM * keys)
    return pl.pallas_call(
        functools.partial(attend_kernel, tick, sub),
        out_shape=(
            jax.ShapeDtypeStruct((rows, n_heads * HEAD_DIM), jnp.bfloat16),
            jax.ShapeDtypeStruct(kin.shape, jnp.bfloat16),
            jax.ShapeDtypeStruct(vin.shape, jnp.bfloat16),
        ),
        in_specs=[pl.BlockSpec(memory_space=pltpu.SMEM)]
        + [vm] * 11,
        out_specs=(vm, vm, vm),
        scratch_shapes=[
            pltpu.VMEM((n_heads * rows, 3 * HEAD_DIM), jnp.bfloat16),
            pltpu.VMEM((keys, 3 * HEAD_DIM), jnp.bfloat16),
            pltpu.VMEM((keys, HEAD_DIM), jnp.bfloat16),
            pltpu.VMEM((rows, keys), jnp.float32),
            pltpu.VMEM((n_heads * rows, keys), jnp.float32),
            pltpu.VMEM((n_heads * rows, keys), jnp.bfloat16),
            pltpu.VMEM((n_heads * rows, HEAD_DIM), jnp.float32),
        ],
        compiler_params=pltpu.CompilerParams(vmem_limit_bytes=VMEM_LIMIT),
        cost_estimate=pl.CostEstimate(
            flops=flops, bytes_accessed=2 * 4 * part * cols, transcendentals=0
        ),
        name="attend",
    )(scal, *pieces, gain, cos_t, sin_t, kv, kin, vin, w)


def project_kernel(
    tick, sub, sections, carried, scal, h0, h1, h2, h3, own, g, hid_in, *refs
):
    following, attn_out, hidden_out, a_vm, o_vm, out_sems, next_sem = refs[carried:]
    pieces = (h0, h1, h2, h3)
    rows = own.shape[0]
    depth = h0.shape[1]
    slots = hid_in.shape[0] // STRETCH
    slot = tick - scal[0]
    valid = (slot >= 0) & (slot < slots)
    alive = (slot < scal[2]).astype(jnp.int32)
    attn = None
    for k in range(4):
        src = pl.multiple_of(scal[3 + k] * depth, depth)
        term = jnp.dot(
            pieces[k][...], g[pl.ds(src, depth), :], preferred_element_type=jnp.float32
        )
        attn = term if attn is None else attn + term
    hid = (own[...].astype(jnp.float32) + attn).astype(jnp.bfloat16)
    live = jnp.broadcast_to(alive, attn.shape) != 0
    a_vm[...] = jnp.where(live, attn, 0.0).astype(jnp.bfloat16)
    o_vm[...] = jnp.where(live, hid.astype(jnp.float32), 0.0).astype(jnp.bfloat16)
    following[...] = hid

    if tick + 1 < slots:

        @pl.when(scal[0] == sections - 1)
        def _():
            nxt = (tick + 1) * STRETCH + sub * rows
            cp = pltpu.make_async_copy(hid_in.at[pl.ds(nxt, rows), :], following, next_sem)
            cp.start()
            cp.wait()

    @pl.when(valid)
    def _():
        row0 = pl.multiple_of(jnp.clip(slot, 0, slots - 1) * STRETCH + sub * rows, rows)
        c1 = pltpu.make_async_copy(a_vm, attn_out.at[pl.ds(row0, rows), :], out_sems.at[0])
        c2 = pltpu.make_async_copy(o_vm, hidden_out.at[pl.ds(row0, rows), :], out_sems.at[1])
        c1.start()
        c2.start()
        c1.wait()
        c2.wait()


def project(tick, sub, sections, scal, heads, own, hid_in, g, attn_buf, hid_buf):
    rows, part = own.shape
    vm = pl.BlockSpec(memory_space=pltpu.VMEM)
    hbm = pl.BlockSpec(memory_space=pltpu.HBM)
    depth = g.shape[0] // 4
    carried = () if attn_buf is None else (attn_buf, hid_buf)
    return pl.pallas_call(
        functools.partial(project_kernel, tick, sub, sections, len(carried)),
        out_shape=(
            jax.ShapeDtypeStruct((rows, part), jnp.bfloat16),
            jax.ShapeDtypeStruct(hid_in.shape, jnp.bfloat16),
            jax.ShapeDtypeStruct(hid_in.shape, jnp.bfloat16),
        ),
        in_specs=[pl.BlockSpec(memory_space=pltpu.SMEM)] + [vm] * 6
        + [hbm] * (1 + len(carried)),
        out_specs=(vm, hbm, hbm),
        input_output_aliases={8: 1, 9: 2} if carried else {},
        scratch_shapes=[
            pltpu.VMEM((rows, part), jnp.bfloat16),
            pltpu.VMEM((rows, part), jnp.bfloat16),
            pltpu.SemaphoreType.DMA((2,)),
            pltpu.SemaphoreType.DMA,
        ],
        compiler_params=pltpu.CompilerParams(vmem_limit_bytes=VMEM_LIMIT),
        cost_estimate=pl.CostEstimate(
            flops=2 * rows * 4 * depth * part, bytes_accessed=2 * 4 * depth * part, transcendentals=0
        ),
        name="project",
    )(scal, *heads, own, g, hid_in, *carried)


def shards(hidden_in, kv_cache, norm_gain, w_query, w_keyval, w_out, stretch_count, prefix_len):
    section_idx = lax.axis_index("section")
    section_total = lax.axis_size("section")
    tensor_idx = lax.axis_index("tensor")
    tensor_total = lax.axis_size("tensor")
    dp_total = lax.axis_size("dp")
    rows_all, part = hidden_in.shape
    dp_idx = lax.axis_index("dp")
    per = dp_total // tensor_total
    block = w_query.shape[1]
    w_local = jnp.concatenate([w_query[0], w_keyval[0, :, 0], w_keyval[0, :, 1]], axis=1)
    w_in = lax.all_gather(w_local, "dp", axis=0, tiled=True)
    w_in, w_out, hidden_in = lax.optimization_barrier((w_in, w_out, hidden_in))
    depth, narrow = w_out.shape[1:]
    piece = depth // per
    received = []
    for k in range(per):
        pairs = []
        for d in range(dp_total):
            for t in range(tensor_total):
                p = (d % per + k) % per
                pairs.append((d * tensor_total + t, (t * per + p) * tensor_total + d // per))
        cut = lax.dynamic_slice_in_dim(w_out[0], (dp_idx % per + k) % per * piece, piece, 0)
        received.append(lax.ppermute(cut, ("dp", "tensor"), pairs))
    received = jnp.stack(received)
    g_local = jnp.concatenate(
        [
            lax.dynamic_index_in_dim(received, (dp_idx % per - c) % per, 0, keepdims=False)
            for c in range(per)
        ],
        axis=1,
    )

    rows = STRETCH // SUBS
    owns = [hidden_in[i * rows : (i + 1) * rows] for i in range(SUBS)]
    first = [spread(own, "tensor") for own in owns]
    g_local, first = lax.optimization_barrier((g_local, first))
    g = lax.all_gather(g_local, "dp", axis=0, tiled=True)

    order = [(tensor_idx - k) % tensor_total for k in range(tensor_total)]
    gain = norm_gain[0].reshape(tensor_total, 1, part)
    gain = jnp.concatenate([lax.dynamic_slice_in_dim(gain, o, 1, 0) for o in order], axis=0)
    prefix = prefix_len[0]
    meta = jnp.stack([section_idx, prefix, stretch_count[0]] + order)
    half = HEAD_DIM // 2
    inv_freq = theta_base ** (-(jnp.arange(half, dtype=jnp.float32) * 2.0 / HEAD_DIM))
    positions = prefix + jnp.arange(rows_all, dtype=jnp.int32)
    angles = positions.astype(jnp.float32)[:, None] * inv_freq[None, :]
    cos_t = jnp.cos(angles)
    sin_t = jnp.sin(angles)
    cos_t = jnp.concatenate([cos_t, cos_t], axis=1)
    sin_t = jnp.concatenate([-sin_t, sin_t], axis=1)
    kv = kv_cache[0, 0]

    kbuf = jnp.zeros((rows_all, HEAD_DIM), jnp.bfloat16)
    vbuf = jnp.zeros((rows_all, HEAD_DIM), jnp.bfloat16)
    attn_buf = hid_buf = None
    slot_total = rows_all // STRETCH
    tick_total = slot_total + section_total - 1
    for tick in range(tick_total):
        for sub in range(SUBS):
            own = owns[sub]
            pieces = spread(own, "tensor") if tick else first[sub]
            heads, kbuf, vbuf = attend(
                tick, sub, meta, pieces, gain, cos_t, sin_t, kv, kbuf, vbuf, w_in
            )
            head_pieces = spread(heads, "tensor")
            following, attn_buf, hid_buf = project(
                tick, sub, section_total, meta, head_pieces, own, hidden_in, g, attn_buf, hid_buf
            )
            if tick + 1 < tick_total:
                owns[sub] = shift(following, "section", 1)
    return (attn_buf[None], hid_buf[None])


def solution(mesh):
    return jax.shard_map(
        shards,
        mesh=mesh,
        in_specs=(
            P("dp", "tensor"),
            P("section", "dp", None, None, "tensor"),
            P("section", None),
            P("section", "dp", "tensor"),
            P("section", "dp", None, "tensor"),
            P("section", "tensor", "dp"),
            P("dp"),
            P("dp"),
        ),
        out_specs=(P("section", "dp", "tensor"), P("section", "dp", "tensor")),
        check_vma=False,
    )
```

```python
import functools

import jax
import jax.numpy as jnp
from jax import lax
from jax.experimental import pallas as pl
from jax.experimental.pallas import tpu as pltpu
from jax.sharding import PartitionSpec as P

HEAD_DIM = 128
STRETCH = 128
SUBS = 2

theta_base = 1000000.0
eps_norm = 1e-06
masked_score = -1e30
score_scale = HEAD_DIM**-0.5 * 1.4426950408889634
VMEM_LIMIT = 36 * 2**20


def shift(value, axis, steps):
    count = lax.axis_size(axis)
    return lax.ppermute(value, axis, [(i, (i + steps) % count) for i in range(count)])


def spread(value, axis):
    return [value] + [shift(value, axis, k) for k in range(1, lax.axis_size(axis))]


def attend_kernel(
    tick, sub, scal, x0, x1, x2, x3, gain, cos_t, sin_t, kv, kin, vin, w,
    heads, kout, vout, q_vm, k_vm, v_vm, bias_vm, s_vm, p_vm, d_vm,
):
    pieces = (x0, x1, x2, x3)
    rows, part = x0.shape
    slots = kin.shape[0] // STRETCH
    slot = jnp.clip(tick - scal[0], 0, slots - 1)
    row0 = pl.multiple_of(slot * STRETCH + sub * rows, rows)
    prefix = scal[1]
    cap = kv.shape[1]
    new_rows = kin.shape[0]
    for j in range(3):
        k_vm[:cap, j * HEAD_DIM : (j + 1) * HEAD_DIM] = kv[0]
    v_vm[:cap, :] = kv[1]
    kept = lax.broadcasted_iota(jnp.int32, (rows, cap), 1) < prefix
    bias_vm[:, :cap] = jnp.where(kept, 0.0, masked_score)
    fresh = lax.broadcasted_iota(jnp.int32, (rows, new_rows), 1) <= (
        row0 + lax.broadcasted_iota(jnp.int32, (rows, new_rows), 0)
    )
    bias_vm[:, cap:] = jnp.where(fresh, 0.0, masked_score)
    kout[...] = kin[...]
    vout[...] = vin[...]
    total = None
    for k in range(4):
        xf = pieces[k][...].astype(jnp.float32)
        part_sum = jnp.sum(xf * xf, axis=1, keepdims=True)
        total = part_sum if total is None else total + part_sum
    scale = lax.rsqrt(total / (4 * part) + eps_norm)
    acc = None
    for k in range(4):
        normed = (pieces[k][...].astype(jnp.float32) * scale * gain[k]).astype(jnp.bfloat16)
        src = pl.multiple_of(scal[3 + k] * part, part)
        term = jnp.dot(normed, w[pl.ds(src, part), :], preferred_element_type=jnp.float32)
        acc = term if acc is None else acc + term
    cosv = cos_t[pl.ds(row0, rows), :]
    sinv = sin_t[pl.ds(row0, rows), :]
    n_heads = heads.shape[1] // HEAD_DIM

    def rot(v):
        return v * cosv + pltpu.roll(v, HEAD_DIM // 2, 1) * sinv

    for h in range(n_heads):
        qh = rot(acc[:, h * HEAD_DIM : (h + 1) * HEAD_DIM]) * score_scale
        hi = qh.astype(jnp.bfloat16)
        rem = qh - hi.astype(jnp.float32)
        mid = rem.astype(jnp.bfloat16)
        low = (rem - mid.astype(jnp.float32)).astype(jnp.bfloat16)
        q_vm[h * rows : (h + 1) * rows, :HEAD_DIM] = hi
        q_vm[h * rows : (h + 1) * rows, HEAD_DIM : 2 * HEAD_DIM] = mid
        q_vm[h * rows : (h + 1) * rows, 2 * HEAD_DIM :] = low
    base = n_heads * HEAD_DIM
    kout[pl.ds(row0, rows), :] = rot(acc[:, base : base + HEAD_DIM]).astype(jnp.bfloat16)
    vout[pl.ds(row0, rows), :] = acc[:, base + HEAD_DIM :].astype(jnp.bfloat16)
    for j in range(3):
        k_vm[cap:, j * HEAD_DIM : (j + 1) * HEAD_DIM] = kout[...]
    v_vm[cap:, :] = vout[...]
    s_vm[...] = lax.dot_general(
        q_vm[...], k_vm[...], (((1,), (1,)), ((), ())), preferred_element_type=jnp.float32
    )
    step = rows

    def softmax(i, carry):
        r = pl.multiple_of(i * step, step)
        b = pl.multiple_of(lax.rem(i * step, rows), step)
        s = s_vm[pl.ds(r, step), :] + bias_vm[pl.ds(b, step), :]
        e = jnp.exp2(s - jnp.max(s, axis=1, keepdims=True))
        d_vm[pl.ds(r, step), :] = jnp.broadcast_to(
            1.0 / jnp.sum(e, axis=1, keepdims=True), (step, HEAD_DIM)
        )
        p_vm[pl.ds(r, step), :] = e.astype(jnp.bfloat16)
        return carry

    lax.fori_loop(0, n_heads * rows // step, softmax, 0, unroll=True)
    out = jnp.dot(p_vm[...], v_vm[...], preferred_element_type=jnp.float32) * d_vm[...]
    for h in range(n_heads):
        heads[:, h * HEAD_DIM : (h + 1) * HEAD_DIM] = out[h * rows : (h + 1) * rows].astype(
            jnp.bfloat16
        )


def attend(tick, sub, scal, pieces, gain, cos_t, sin_t, kv, kin, vin, w):
    rows, part = pieces[0].shape
    cols = w.shape[1]
    n_heads = cols // HEAD_DIM - 2
    keys = kv.shape[1] + kin.shape[0]
    vm = pl.BlockSpec(memory_space=pltpu.VMEM)
    flops = 2 * rows * (4 * part * cols + 4 * n_heads * HEAD_DIM * keys)
    return pl.pallas_call(
        functools.partial(attend_kernel, tick, sub),
        out_shape=(
            jax.ShapeDtypeStruct((rows, n_heads * HEAD_DIM), jnp.bfloat16),
            jax.ShapeDtypeStruct(kin.shape, jnp.bfloat16),
            jax.ShapeDtypeStruct(vin.shape, jnp.bfloat16),
        ),
        in_specs=[pl.BlockSpec(memory_space=pltpu.SMEM)]
        + [vm] * 11,
        out_specs=(vm, vm, vm),
        scratch_shapes=[
            pltpu.VMEM((n_heads * rows, 3 * HEAD_DIM), jnp.bfloat16),
            pltpu.VMEM((keys, 3 * HEAD_DIM), jnp.bfloat16),
            pltpu.VMEM((keys, HEAD_DIM), jnp.bfloat16),
            pltpu.VMEM((rows, keys), jnp.float32),
            pltpu.VMEM((n_heads * rows, keys), jnp.float32),
            pltpu.VMEM((n_heads * rows, keys), jnp.bfloat16),
            pltpu.VMEM((n_heads * rows, HEAD_DIM), jnp.float32),
        ],
        compiler_params=pltpu.CompilerParams(vmem_limit_bytes=VMEM_LIMIT),
        cost_estimate=pl.CostEstimate(
            flops=flops, bytes_accessed=2 * 4 * part * cols, transcendentals=0
        ),
        name="attend",
    )(scal, *pieces, gain, cos_t, sin_t, kv, kin, vin, w)


def project_kernel(
    tick, sub, sections, carried, scal, h0, h1, h2, h3, own, g, hid_in, *refs
):
    following, attn_out, hidden_out, a_vm, o_vm, out_sems, next_sem = refs[carried:]
    pieces = (h0, h1, h2, h3)
    rows = own.shape[0]
    depth = h0.shape[1]
    slots = hid_in.shape[0] // STRETCH
    slot = tick - scal[0]
    valid = (slot >= 0) & (slot < slots)
    alive = (slot < scal[2]).astype(jnp.int32)
    attn = None
    for k in range(4):
        src = pl.multiple_of(scal[3 + k] * depth, depth)
        term = jnp.dot(
            pieces[k][...], g[pl.ds(src, depth), :], preferred_element_type=jnp.float32
        )
        attn = term if attn is None else attn + term
    hid = (own[...].astype(jnp.float32) + attn).astype(jnp.bfloat16)
    live = jnp.broadcast_to(alive, attn.shape) != 0
    a_vm[...] = jnp.where(live, attn, 0.0).astype(jnp.bfloat16)
    o_vm[...] = jnp.where(live, hid.astype(jnp.float32), 0.0).astype(jnp.bfloat16)
    following[...] = hid

    if tick + 1 < slots:

        @pl.when(scal[0] == sections - 1)
        def _():
            nxt = (tick + 1) * STRETCH + sub * rows
            cp = pltpu.make_async_copy(hid_in.at[pl.ds(nxt, rows), :], following, next_sem)
            cp.start()
            cp.wait()

    @pl.when(valid)
    def _():
        row0 = pl.multiple_of(jnp.clip(slot, 0, slots - 1) * STRETCH + sub * rows, rows)
        c1 = pltpu.make_async_copy(a_vm, attn_out.at[pl.ds(row0, rows), :], out_sems.at[0])
        c2 = pltpu.make_async_copy(o_vm, hidden_out.at[pl.ds(row0, rows), :], out_sems.at[1])
        c1.start()
        c2.start()
        c1.wait()
        c2.wait()


def project(tick, sub, sections, scal, heads, own, hid_in, g, attn_buf, hid_buf):
    rows, part = own.shape
    vm = pl.BlockSpec(memory_space=pltpu.VMEM)
    hbm = pl.BlockSpec(memory_space=pltpu.HBM)
    depth = g.shape[0] // 4
    carried = () if attn_buf is None else (attn_buf, hid_buf)
    return pl.pallas_call(
        functools.partial(project_kernel, tick, sub, sections, len(carried)),
        out_shape=(
            jax.ShapeDtypeStruct((rows, part), jnp.bfloat16),
            jax.ShapeDtypeStruct(hid_in.shape, jnp.bfloat16),
            jax.ShapeDtypeStruct(hid_in.shape, jnp.bfloat16),
        ),
        in_specs=[pl.BlockSpec(memory_space=pltpu.SMEM)] + [vm] * 6
        + [hbm] * (1 + len(carried)),
        out_specs=(vm, hbm, hbm),
        input_output_aliases={8: 1, 9: 2} if carried else {},
        scratch_shapes=[
            pltpu.VMEM((rows, part), jnp.bfloat16),
            pltpu.VMEM((rows, part), jnp.bfloat16),
            pltpu.SemaphoreType.DMA((2,)),
            pltpu.SemaphoreType.DMA,
        ],
        compiler_params=pltpu.CompilerParams(vmem_limit_bytes=VMEM_LIMIT),
        cost_estimate=pl.CostEstimate(
            flops=2 * rows * 4 * depth * part, bytes_accessed=2 * 4 * depth * part, transcendentals=0
        ),
        name="project",
    )(scal, *heads, own, g, hid_in, *carried)


def unfold_kernel(blocks, out):
    _, height, double = blocks.shape
    width = double // 2
    total = out.shape[1] // width
    count = out.shape[0] // (2 * height)
    for t in range(count):
        for half in range(2):
            row = jnp.concatenate(
                [
                    blocks[c * count + t, :, half * width : (half + 1) * width]
                    for c in range(total)
                ],
                axis=1,
            )
            start = (2 * t + half) * height
            out[start : start + height, :] = row


def unfold(blocks, count, per):
    vm = pl.BlockSpec(memory_space=pltpu.VMEM)
    _, height, double = blocks.shape
    return pl.pallas_call(
        unfold_kernel,
        out_shape=jax.ShapeDtypeStruct((2 * count * height, per * double // 2), jnp.bfloat16),
        in_specs=[vm],
        out_specs=vm,
        compiler_params=pltpu.CompilerParams(vmem_limit_bytes=VMEM_LIMIT),
        cost_estimate=pl.CostEstimate(flops=0, bytes_accessed=4 * blocks.size, transcendentals=0),
        name="unfold",
    )(blocks)


def shards(hidden_in, kv_cache, norm_gain, w_query, w_keyval, w_out, stretch_count, prefix_len):
    section_idx = lax.axis_index("section")
    section_total = lax.axis_size("section")
    tensor_idx = lax.axis_index("tensor")
    tensor_total = lax.axis_size("tensor")
    dp_total = lax.axis_size("dp")
    rows_all, part = hidden_in.shape
    dp_idx = lax.axis_index("dp")
    per = dp_total // tensor_total
    block = w_query.shape[1]
    w_local = jnp.concatenate([w_query[0], w_keyval[0, :, 0], w_keyval[0, :, 1]], axis=1)
    pairs = []
    for d in range(dp_total):
        for t in range(tensor_total):
            d2, t2 = d % per * tensor_total + t, d // per
            pairs.append((d * tensor_total + t, d2 * tensor_total + t2))
    w_in = lax.all_gather(w_local, "dp", axis=0, tiled=True)
    moved = lax.ppermute(w_out[0], ("dp", "tensor"), pairs)
    g_local = jnp.concatenate([moved[:block], moved[block:]], axis=1)
    g_local, w_local = lax.optimization_barrier((g_local, w_local))
    blocks = lax.all_gather(g_local, "dp", axis=0, tiled=False)

    order = [(tensor_idx - k) % tensor_total for k in range(tensor_total)]
    gain = norm_gain[0].reshape(tensor_total, 1, part)
    gain = jnp.concatenate([lax.dynamic_slice_in_dim(gain, o, 1, 0) for o in order], axis=0)
    prefix = prefix_len[0]
    meta = jnp.stack([section_idx, prefix, stretch_count[0]] + order)
    half = HEAD_DIM // 2
    inv_freq = theta_base ** (-(jnp.arange(half, dtype=jnp.float32) * 2.0 / HEAD_DIM))
    positions = prefix + jnp.arange(rows_all, dtype=jnp.int32)
    angles = positions.astype(jnp.float32)[:, None] * inv_freq[None, :]
    cos_t = jnp.cos(angles)
    sin_t = jnp.sin(angles)
    cos_t = jnp.concatenate([cos_t, cos_t], axis=1)
    sin_t = jnp.concatenate([-sin_t, sin_t], axis=1)
    kv = kv_cache[0, 0]

    kbuf = jnp.zeros((rows_all, HEAD_DIM), jnp.bfloat16)
    vbuf = jnp.zeros((rows_all, HEAD_DIM), jnp.bfloat16)
    attn_buf = hid_buf = None
    rows = STRETCH // SUBS
    slot_total = rows_all // STRETCH
    tick_total = slot_total + section_total - 1
    owns = [hidden_in[i * rows : (i + 1) * rows] for i in range(SUBS)]
    for tick in range(tick_total):
        for sub in range(SUBS):
            own = owns[sub]
            pieces = spread(own, "tensor")
            heads, kbuf, vbuf = attend(
                tick, sub, meta, pieces, gain, cos_t, sin_t, kv, kbuf, vbuf, w_in
            )
            head_pieces = spread(heads, "tensor")
            if tick + sub == 0:
                blocks, _ = lax.optimization_barrier((blocks, heads))
                g = unfold(blocks, tensor_total, per)
            following, attn_buf, hid_buf = project(
                tick, sub, section_total, meta, head_pieces, own, hidden_in, g, attn_buf, hid_buf
            )
            if tick + 1 < tick_total:
                owns[sub] = shift(following, "section", 1)
    return (attn_buf[None], hid_buf[None])


def solution(mesh):
    return jax.shard_map(
        shards,
        mesh=mesh,
        in_specs=(
            P("dp", "tensor"),
            P("section", "dp", None, None, "tensor"),
            P("section", None),
            P("section", "dp", "tensor"),
            P("section", "dp", None, "tensor"),
            P("section", "tensor", "dp"),
            P("dp"),
            P("dp"),
        ),
        out_specs=(P("section", "dp", "tensor"), P("section", "dp", "tensor")),
        check_vma=False,
    )
```
